128 devices in a mesh: width: 4 (over z), row: 4 (over y), src: 8 (over x, core).
Axes of the slice: x: 4, y: 4, z: 4, core: 2. Of those that a mesh axis runs over, the one named last changes fastest.
Arguments:
- query_rows: bfloat16 [1024, 8192], P('row', 'width'), may hold values from -150 to 150
- key_rows: bfloat16 [1024, 1024], P('src', 'width'), may hold values from -7 to 7
- value_rows: bfloat16 [1024, 1024], P('src'), may hold values from -6 to 6
- out_proj: bfloat16 [8192, 8192], P(('row', 'src'), 'width'), may hold values from -0.0625 to 0.0625
Outputs:
- share: float32 [1024, 1024], P('row', ('src', 'width'))
The draws below stay inside these ranges and needn't reach their ends.
All inputs are finite; a program needn't handle non-finite values.
Results may differ from the reference program's by a relative error of at most 0.0014.
Values may be sent and summed in bfloat16 or wider, within the bound.
A program may use at most 192 MiB of HBM per device.

```python
import jax
import jax.numpy as jnp
from jax import lax

D = 8192
H = 64
KV = 8
HD = 128
SEQ = 1024


def final_keys(key):
    normal_keys = jnp.clip(jax.random.normal(jax.random.fold_in(key, 11), (SEQ, KV * HD), jnp.float32), -6.0, 6.0)
    return normal_keys


def draw_key_rows(key, part):
    return final_keys(key).astype(jnp.bfloat16)


def draw_query_rows(key, part):
    result = jnp.clip(jax.random.normal(jax.random.fold_in(key, 21), (SEQ, H * HD), jnp.float32), -6.0, 6.0)
    return result.astype(jnp.bfloat16)


def block_scale(own_key, shape, shards, smallest, high):
    gain = 1.0
    for axis_at, shards_of in shards:
        draws = jax.random.uniform(jax.random.fold_in(jax.random.fold_in(own_key, 6), axis_at), (shards_of,), jnp.float32, smallest / len(shards), high / len(shards))
        gain = gain * jnp.repeat(jnp.exp(draws), shape[axis_at] // shards_of).reshape((-1,) + (1,) * (len(shape) - 1 - axis_at))
    return gain


def bell_draw(key, dims, spread, reach, cuts=(), kind=jnp.bfloat16):
    level = block_scale(key, dims, cuts, -0.22, 0.18) if cuts else 1.0
    array = jax.random.normal(key, dims, jnp.float32) * spread * level
    return jnp.minimum(jnp.maximum(array, -reach), reach).astype(kind)


def setup_inputs(seed: int = 0) -> dict:
    key_of = jax.random.split(jax.random.key(seed), 5)
    return {
        "query_rows": draw_query_rows(jax.random.fold_in(key_of[4], 71), 0),
        "key_rows": draw_key_rows(jax.random.fold_in(key_of[4], 71), 0),
        "value_rows": bell_draw(key_of[2], (SEQ, KV * HD), 1.0, 6.0, ((0, 8),)),
        "out_proj": bell_draw(key_of[3], (H * HD, D), (H * HD) ** -0.5, 0.0625, ((0, 32), (1, 4))),
    }


def reference(query_rows, key_rows, value_rows, out_proj):
    group_size = H // KV
    queries = query_rows.astype(jnp.float32).reshape(SEQ, KV, group_size, HD)
    key_heads = key_rows.astype(jnp.float32).reshape(SEQ, KV, HD)
    scores = jnp.einsum('ikgd,jkd->kgij', queries, key_heads).reshape(H, SEQ, SEQ) / jnp.sqrt(jnp.float32(HD))
    positions = jnp.arange(SEQ, dtype=jnp.int32)
    causal = positions[:, None] >= positions[None, :]
    masked = jnp.where(causal, scores, jnp.float32(-1e+30))
    row_peak = lax.optimization_barrier(jnp.max(masked, axis=-1, keepdims=True))
    shifted = jnp.where(causal, jnp.exp(masked - row_peak), jnp.float32(0.0))
    weights = (shifted / lax.optimization_barrier(jnp.sum(shifted, axis=-1, keepdims=True))).astype(jnp.bfloat16)
    value_heads = value_rows.astype(jnp.float32).reshape(SEQ, KV, HD)
    proj_heads = out_proj.astype(jnp.float32).reshape(KV, group_size, HD, D)

    def image_one(kv_index):
        value_kv = jnp.take(value_heads, kv_index, axis=1)
        weight_kv = jnp.take(proj_heads, kv_index, axis=0)
        return jnp.einsum('jd,gde->jge', value_kv, weight_kv).astype(jnp.bfloat16)
    images = lax.map(image_one, jnp.arange(KV, dtype=jnp.int32))
    images = images.transpose(1, 0, 2, 3).reshape(SEQ, H, D)
    blocks = SEQ // 8
    weight_blocks = weights.reshape(H, SEQ, blocks, 8).transpose(2, 0, 1, 3)
    image_blocks = images.reshape(blocks, 8, H, D)

    def norm_block(operands):
        attend, source_images = operands
        contrib = jnp.einsum('hij,jhe->jie', attend.astype(jnp.float32), source_images.astype(jnp.float32))
        return lax.optimization_barrier(jnp.sum(jnp.abs(contrib), axis=-1))
    norms_table = lax.map(norm_block, (weight_blocks, image_blocks)).reshape(SEQ, SEQ).T
    totals = lax.optimization_barrier(jnp.sum(norms_table, axis=1, keepdims=True))
    return (positions + 1).astype(jnp.float32)[:, None] * norms_table / totals
```

```python
import math
import jax, jax.numpy as jnp
from jax import lax
from jax.experimental import pallas as pl
from jax.experimental.pallas import tpu as pltpu
from jax.sharding import PartitionSpec as PS_
C2 = math.log2(math.e) / math.sqrt(128.0)
F32, BF = jnp.float32, jnp.bfloat16
NEG = -1e30
PS, IS = 17, 65

def pair_of(y):
    return jnp.where(y == 0, 0, jnp.where(y == 3, 1, y + 1))

def kernel_b(q, k, v, o, out, P, W, MS, LS, FS, IM):
    p = pair_of(lax.axis_index("row"))
    big = 7 - p
    jl = lax.broadcasted_iota(jnp.int32, (128, 256), 0)
    il = lax.broadcasted_iota(jnp.int32, (128, 256), 1) % 128

    def scores(zc, slot, ib, base):
        MS[...] = jnp.full(MS.shape, NEG, F32)
        LS[...] = jnp.zeros(LS.shape, F32)

        def block(jb, diag):
            for hp in range(8):
                kk = k[zc, pl.ds(pl.multiple_of(jb * 128, 128), 128), (hp // 4) * 128:(hp // 4 + 1) * 128]
                qq = jnp.concatenate([q[zc, slot * 128:(slot + 1) * 128, (2 * hp + a) * 128:(2 * hp + a + 1) * 128] for a in (0, 1)], axis=0)
                s = lax.dot_general(kk, qq, (((1,), (1,)), ((), ())), preferred_element_type=F32)
                if diag:
                    s = jnp.where(jl <= il, s, NEG)
                m = jnp.max(s, axis=0, keepdims=True)
                e = jnp.exp2((s - m) * C2)
                l = jnp.sum(e, axis=0, keepdims=True)
                for a in (0, 1):
                    lanes = slice(a * 128, (a + 1) * 128)
                    P[jb, pl.ds(2 * hp + a, 128, stride=PS), :] = e[:, lanes]
                    MS[jb, 2 * hp + a:2 * hp + a + 1, :] = m[:, lanes]
                    LS[jb, 2 * hp + a:2 * hp + a + 1, :] = l[:, lanes]

        def plain(jb, c):
            block(jb, False)
            return c
        lax.fori_loop(0, ib, plain, 0)
        block(ib, True)
        ms = MS[...]
        f = jnp.exp2((ms - jnp.max(ms, axis=0, keepdims=True)) * C2)
        z = jnp.sum(f * LS[...], axis=0, keepdims=True)
        FS[...] = f / z

        def conv(jb, c):
            f = FS[jb]
            for j in range(128):
                x = P[jb, j * PS:j * PS + 16, :] * f
                W[base + jb, j, pl.ds(pl.multiple_of(zc * 16, 16), 16), :] = x.astype(BF)
            return c
        lax.fori_loop(0, ib + 1, conv, 0)

    def zstep(zc, c):
        scores(zc, 0, p, big + 1)
        scores(zc, 1, big, 0)
        return c
    lax.fori_loop(0, 4, zstep, 0)

    out[...] = jnp.zeros(out.shape, F32)

    def jstep(jb, c):
        def img(g, c):
            vvs = [v[pl.ds(pl.multiple_of(jb * 128, 128), 128), pl.ds(pl.multiple_of(g * 256 + b * 128, 128), 128)] for b in (0, 1)]
            for hh in range(16):
                h = g * 16 + hh
                oo = o[pl.ds(pl.multiple_of(h * 128, 128), 128), :]
                x = jnp.dot(vvs[hh // 8], oo, preferred_element_type=F32)
                for a in (0, 1):
                    IM[a, pl.ds(h, 128, stride=IS), :] = x[:, a * 128:(a + 1) * 128]
            return c
        lax.fori_loop(0, 4, img, 0)

        def contrib(t, slot):
            zero = jnp.zeros((64, 128), BF)
            PU = 32

            def pairs(n, c):
                rows = []
                for u in range(PU):
                    j = n * (2 * PU) + 2 * u
                    r0 = pl.multiple_of(n * (2 * PU * IS), 8)
                    lhs = jnp.concatenate([jnp.concatenate([IM[a, pl.ds(r0 + (2 * u + b) * IS, 64), :].astype(BF) for b in (0, 1)], axis=0) for a in (0, 1)], axis=1)
                    rhs = jnp.concatenate([
                        jnp.concatenate([W[t, j], zero], axis=1),
                        jnp.concatenate([zero, W[t, j + 1]], axis=1)], axis=0)
                    cc = lax.dot_general(lhs, rhs, (((0,), (0,)), ((), ())), preferred_element_type=F32)
                    r = jnp.sum(jnp.abs(cc), axis=0, keepdims=True)
                    rows += [r[:, :128], r[:, 128:]]
                for b in range(PU // 4):
                    out[slot, pl.ds(pl.multiple_of(jb * 128 + n * (2 * PU) + 8 * b, 8), 8), :] = jnp.concatenate(rows[8 * b:8 * b + 8], axis=0)
                return c
            lax.fori_loop(0, 128 // (2 * PU), pairs, 0)
        contrib(jb, 1)

        @pl.when(jb <= p)
        def _():
            contrib(big + 1 + jb, 0)
        return c
    lax.fori_loop(0, big + 1, jstep, 0)

SCR = [pltpu.VMEM((8, 128 * PS, 128), F32), pltpu.VMEM((9, 128, 64, 128), BF),
       pltpu.VMEM((8, 16, 128), F32), pltpu.VMEM((8, 16, 128), F32), pltpu.VMEM((8, 16, 128), F32),
       pltpu.VMEM((2, 128 * IS, 128), F32)]


def contributions(q, k, v, o):
    vm = pl.BlockSpec(memory_space=pltpu.VMEM)
    return pl.pallas_call(kernel_b, out_shape=jax.ShapeDtypeStruct((2, 1024, 128), F32),
        in_specs=[vm] * 4, out_specs=vm, scratch_shapes=SCR,
        compiler_params=pltpu.CompilerParams(vmem_limit_bytes=62 * 2**20))(q, k, v, o)


PARTNER = [(0, 3), (3, 0), (1, 2), (2, 1)]


def body(query_rows, key_rows, value_rows, out_proj):
    row = lax.axis_index("row")
    low = row < 2
    kept, other = query_rows[:128], lax.ppermute(query_rows[128:], "row", PARTNER)
    small, big = jnp.where(low, kept, other), jnp.where(low, other, kept)
    q = lax.all_gather(jnp.concatenate([small, big], axis=0), "width")
    k = lax.all_gather(lax.all_gather(key_rows, "src", tiled=True), "width")
    v = lax.all_gather(value_rows, "src", tiled=True)
    o = lax.all_to_all(out_proj, "src", 1, 0, tiled=True)
    o = lax.all_gather(o, "row", tiled=True)
    part = contributions(q, k, v, o)
    norms = lax.psum_scatter(part, ("src", "width"), scatter_dimension=1, tiled=True)
    totals = lax.psum(jnp.sum(norms, axis=1), ("src", "width"))
    p = pair_of(row)
    pos = jnp.stack([p, 7 - p])[:, None] * 128 + jnp.arange(1, 129, dtype=jnp.int32)[None, :]
    share = norms * (pos.astype(F32) / totals)[:, None, :]
    share = share.transpose(0, 2, 1)
    kept, other = jnp.where(low, share[0], share[1]), jnp.where(low, share[1], share[0])
    return jnp.concatenate([kept, lax.ppermute(other, "row", PARTNER)], axis=0)


def solution(mesh):
    placed = (PS_("row", "width"), PS_("src", "width"), PS_("src", None), PS_(("row", "src"), "width"))
    return jax.shard_map(
        body, mesh=mesh, in_specs=placed, out_specs=PS_("row", ("src", "width")), check_vma=False
    )
```

```python
import math
import jax, jax.numpy as jnp
from jax import lax
from jax.experimental import pallas as pl
from jax.experimental.pallas import tpu as pltpu
from jax.sharding import PartitionSpec as PS_
C2 = math.log2(math.e) / math.sqrt(128.0)
F32, BF = jnp.float32, jnp.bfloat16
NEG = -1e30
PS, IS = 17, 65

def pair_of(y):
    return jnp.where(y == 0, 0, jnp.where(y == 3, 1, y + 1))

def kernel_b(q, k, v, o, out, P, W, MS, LS, FS, IM):
    p = pair_of(lax.axis_index("row"))
    big = 7 - p
    jl = lax.broadcasted_iota(jnp.int32, (128, 256), 0)
    il = lax.broadcasted_iota(jnp.int32, (128, 256), 1) % 128

    def scores(zc, slot, ib, base):
        MS[...] = jnp.full(MS.shape, NEG, F32)
        LS[...] = jnp.zeros(LS.shape, F32)

        def block(jb, diag):
            for hp in range(8):
                kk = k[zc, pl.ds(pl.multiple_of(jb * 128, 128), 128), (hp // 4) * 128:(hp // 4 + 1) * 128]
                qq = jnp.concatenate([q[zc, slot, :, (2 * hp + a) * 128:(2 * hp + a + 1) * 128] for a in (0, 1)], axis=0)
                s = lax.dot_general(kk, qq, (((1,), (1,)), ((), ())), preferred_element_type=F32)
                if diag:
                    s = jnp.where(jl <= il, s, NEG)
                m = jnp.max(s, axis=0, keepdims=True)
                e = jnp.exp2((s - m) * C2)
                l = jnp.sum(e, axis=0, keepdims=True)
                for a in (0, 1):
                    lanes = slice(a * 128, (a + 1) * 128)
                    P[jb, pl.ds(2 * hp + a, 128, stride=PS), :] = e[:, lanes]
                    MS[jb, 2 * hp + a:2 * hp + a + 1, :] = m[:, lanes]
                    LS[jb, 2 * hp + a:2 * hp + a + 1, :] = l[:, lanes]

        def plain(jb, c):
            block(jb, False)
            return c
        lax.fori_loop(0, ib, plain, 0)
        block(ib, True)
        ms = MS[...]
        f = jnp.exp2((ms - jnp.max(ms, axis=0, keepdims=True)) * C2)
        z = jnp.sum(f * LS[...], axis=0, keepdims=True)
        FS[...] = f / z

        def conv(jb, c):
            f = FS[jb]
            for j in range(128):
                x = P[jb, j * PS:j * PS + 16, :] * f
                W[base + jb, j, pl.ds(pl.multiple_of(zc * 16, 16), 16), :] = x.astype(BF)
            return c
        lax.fori_loop(0, ib + 1, conv, 0)

    def zstep(zc, c):
        scores(zc, 0, p, big + 1)
        scores(zc, 1, big, 0)
        return c
    lax.fori_loop(0, 4, zstep, 0)

    out[...] = jnp.zeros(out.shape, F32)

    def jstep(jb, c):
        def img(g, c):
            vvs = [v[pl.ds(pl.multiple_of(jb * 128, 128), 128), pl.ds(pl.multiple_of(g * 256 + b * 128, 128), 128)] for b in (0, 1)]
            for hh in range(16):
                h = g * 16 + hh
                oo = jnp.concatenate([o[a, pl.ds(pl.multiple_of(h * 128, 128), 128), :] for a in (0, 1)], axis=1)
                x = jnp.dot(vvs[hh // 8], oo, preferred_element_type=F32)
                for a in (0, 1):
                    IM[a, pl.ds(h, 128, stride=IS), :] = x[:, a * 128:(a + 1) * 128]
            return c
        lax.fori_loop(0, 4, img, 0)

        def contrib(t, slot):
            zero = jnp.zeros((64, 128), BF)
            PU = 32

            def pairs(n, c):
                rows = []
                for u in range(PU):
                    j = n * (2 * PU) + 2 * u
                    r0 = pl.multiple_of(n * (2 * PU * IS), 8)
                    lhs = jnp.concatenate([jnp.concatenate([IM[a, pl.ds(r0 + (2 * u + b) * IS, 64), :].astype(BF) for b in (0, 1)], axis=0) for a in (0, 1)], axis=1)
                    rhs = jnp.concatenate([
                        jnp.concatenate([W[t, j], zero], axis=1),
                        jnp.concatenate([zero, W[t, j + 1]], axis=1)], axis=0)
                    cc = lax.dot_general(lhs, rhs, (((0,), (0,)), ((), ())), preferred_element_type=F32)
                    r = jnp.sum(jnp.abs(cc), axis=0, keepdims=True)
                    rows += [r[:, :128], r[:, 128:]]
                for b in range(PU // 4):
                    out[slot, pl.ds(pl.multiple_of(jb * 128 + n * (2 * PU) + 8 * b, 8), 8), :] = jnp.concatenate(rows[8 * b:8 * b + 8], axis=0)
                return c
            lax.fori_loop(0, 128 // (2 * PU), pairs, 0)
        contrib(jb, 1)

        @pl.when(jb <= p)
        def _():
            contrib(big + 1 + jb, 0)
        return c
    lax.fori_loop(0, big + 1, jstep, 0)

SCR = [pltpu.VMEM((8, 128 * PS, 128), F32), pltpu.VMEM((9, 128, 64, 128), BF),
       pltpu.VMEM((8, 16, 128), F32), pltpu.VMEM((8, 16, 128), F32), pltpu.VMEM((8, 16, 128), F32),
       pltpu.VMEM((2, 128 * IS, 128), F32)]


def contributions(q, k, v, o):
    vm = pl.BlockSpec(memory_space=pltpu.VMEM)
    return pl.pallas_call(kernel_b, out_shape=jax.ShapeDtypeStruct((2, 1024, 128), F32),
        in_specs=[vm] * 4, out_specs=vm, scratch_shapes=SCR,
        compiler_params=pltpu.CompilerParams(vmem_limit_bytes=62 * 2**20))(q, k, v, o)


MESH = pl.DeviceIdType.MESH


class Links:
    def __init__(self, send, recv, at=None):
        self.send, self.recv, self.n, self.at = send, recv, 0, at

    def to(self, source, target, **where):
        i = self.n
        self.n += 1
        return pltpu.make_async_remote_copy(src_ref=source, dst_ref=target, send_sem=self.send.at[i], recv_sem=self.recv.at[i],
                                            device_id={**self.at, **where}, device_id_type=MESH)


def start_all(copies):
    for cp in copies:
        cp.start()
    return copies


def gather_kernel(q, k, v, o, Q, K, V, OC, send, recv, local):
    z, y, s = lax.axis_index("width"), lax.axis_index("row"), lax.axis_index("src")
    x, c = s // 2, s % 2
    at = {"width": z, "row": y, "src": s}
    zu, zd, zf = (z + 1) % 4, (z + 3) % 4, (z + 2) % 4
    yu, yd, yf = (y + 1) % 4, (y + 3) % 4, (y + 2) % 4
    xu, xd, xf = (x + 1) % 4, (x + 3) % 4, (x + 2) % 4
    su, sd, sib = xu * 2 + c, xd * 2 + c, x * 2 + 1 - c
    partner = 3 - y
    tslot = y // 2

    barrier = pltpu.get_barrier_semaphore()

    def greet(**where):
        pl.semaphore_signal(barrier, inc=1, device_id={**at, **where}, device_id_type=MESH)

    greet(width=zu)
    greet(width=zd)
    greet(row=yu)
    greet(row=yd)
    for d in range(1, 8):
        greet(src=(s + d) % 8)
    pl.semaphore_wait(barrier, 11)

    links = Links(send, recv, at)
    to = links.to
    mine = pl.ds(s * 128, 128)

    def ksl(a):
        return pl.ds(a * 128, 128)

    swap = to(q.at[pl.ds(128, 128), :], Q.at[z, c], row=partner)
    loc_q = pltpu.make_async_copy(q.at[pl.ds(0, 128), :], Q.at[z, c], local.at[0])

    @pl.when(c == tslot)
    def _():
        swap.start()
        loc_q.start()

    locs = [pltpu.make_async_copy(k, K.at[z, mine, :], local.at[1]),
            pltpu.make_async_copy(v, V.at[mine, :], local.at[2])]
    locs += [pltpu.make_async_copy(o.at[:, pl.ds(s * 256 + ch * 128, 128)], OC.at[ch, pl.ds((y * 8 + s) * 256, 256), :], local.at[3 + ch]) for ch in (0, 1)]
    start_all(locs)
    kz = start_all([to(k, K.at[z, mine, :], width=w) for w in (zu, zd)])
    ox = []
    for ch in (0, 1):
        ox.append(start_all([to(o.at[:, pl.ds(((s + d) % 8) * 256 + ch * 128, 128)], OC.at[ch, pl.ds((y * 8 + s) * 256, 256), :], src=(s + d) % 8) for d in range(1, 8)]))
        if ch == 0:
            vx = start_all([to(v, V.at[mine, :], src=w) for w in (su, sd, sib)])

    @pl.when(c == tslot)
    def _():
        loc_q.wait()

    @pl.when(c != tslot)
    def _():
        swap.wait_recv()

    def qring(ref_of):
        return start_all([to(ref_of, ref_of, width=w) for w in (zu, zd)])

    qz = qring(Q.at[z, c])
    qs = start_all([to(Q.at[z, c], Q.at[z, c], src=sib)])

    def part(ref, lo, n):
        return ref.at[pl.ds(lo, n)]

    kz[0].wait_recv()
    ks = pl.ds(s * 128, 64)
    ks2 = pl.ds(s * 128 + 64, 64)
    kf = [to(K.at[zd, ks, :], K.at[zd, ks, :], width=zu), to(K.at[zu, ks2, :], K.at[zu, ks2, :], width=zd)]
    kf[0].start()
    kz[1].wait_recv()
    kf[1].start()
    for cp in locs:
        cp.wait()
    for cp in kf:
        cp.wait_recv()
    kx = start_all([to(K.at[:, mine, :], K.at[:, mine, :], src=w) for w in (su, sd, sib)])

    def rows(a):
        return pl.ds((a * 2 + c) * 128, 128)

    def vhalf(a, h):
        return V.at[pl.ds((a * 2 + c) * 128 + h * 64, 64), :]

    def khalf(a, h):
        return K.at[pl.ds(h * 2, 2), rows(a), :]

    def onward(first, half, whole):
        first[0].wait_recv()
        f0 = to(half(xd, 0), half(xd, 0), src=su)
        f0.start()
        g0 = to(whole(xd), whole(xd), src=sib)
        g0.start()
        first[1].wait_recv()
        f1 = to(half(xu, 1), half(xu, 1), src=sd)
        f1.start()
        g1 = to(whole(xu), whole(xu), src=sib)
        g1.start()
        return [f0, f1], [g0, g1]

    vf, vg = onward(vx, vhalf, lambda a: V.at[rows(a), :])
    kxf, kg = onward(kx, khalf, lambda a: K.at[:, rows(a), :])

    def orows(ch, a, lo, n):
        return OC.at[ch, pl.ds(a * 2048 + lo, n), :]

    oy = []
    for ch in (0, 1):
        for cp in ox[ch]:
            cp.wait_recv()
        oy.append(start_all([to(orows(ch, y, 0, 2048), orows(ch, y, 0, 2048), row=w) for w in (yu, yd)]))
        if ch == 0:
            qz[0].wait_recv()
            qf = [to(Q.at[zd, c, pl.ds(0, 64)], Q.at[zd, c, pl.ds(0, 64)], width=zu),
                  to(Q.at[zu, c, pl.ds(64, 64)], Q.at[zu, c, pl.ds(64, 64)], width=zd)]
            qf[0].start()
            qs += start_all([to(Q.at[zd, c], Q.at[zd, c], src=sib)])
            qz[1].wait_recv()
            qf[1].start()
            qs += start_all([to(Q.at[zu, c], Q.at[zu, c], src=sib)])
            for cp in vf + kxf:
                cp.wait_recv()
            vg += start_all([to(V.at[rows(xf), :], V.at[rows(xf), :], src=sib)])
            kg += start_all([to(K.at[:, rows(xf), :], K.at[:, rows(xf), :], src=sib)])
    of = []
    for ch in (0, 1):
        oy[ch][0].wait_recv()
        a = to(orows(ch, yd, 0, 1024), orows(ch, yd, 0, 1024), row=yu)
        a.start()
        oy[ch][1].wait_recv()
        b = to(orows(ch, yu, 1024, 1024), orows(ch, yu, 1024, 1024), row=yd)
        b.start()
        of += [a, b]
        if ch == 0:
            for cp in qf:
                cp.wait_recv()
            qs += start_all([to(Q.at[zf, c], Q.at[zf, c], src=sib)])

    for cp in [vx[2], kx[2]] + vg + kg + qs + of:
        cp.wait_recv()
    for cp in kz + ox[0] + ox[1] + vx + qz + qs + kf + kx + vf + vg + kxf + kg + qf + oy[0] + oy[1] + of:
        cp.wait_send()

    @pl.when(c == tslot)
    def _():
        swap.wait_send()


def gather(q, k, v, o):
    vm = pl.BlockSpec(memory_space=pltpu.VMEM)
    hb = pl.BlockSpec(memory_space=pl.ANY)
    return pl.pallas_call(gather_kernel,
        out_shape=[jax.ShapeDtypeStruct((4, 2, 128, 2048), BF), jax.ShapeDtypeStruct((4, 1024, 256), BF),
                   jax.ShapeDtypeStruct((1024, 1024), BF), jax.ShapeDtypeStruct((2, 8192, 128), BF)],
        in_specs=[hb] * 4, out_specs=[vm] * 4,
        scratch_shapes=[pltpu.SemaphoreType.DMA((64,)), pltpu.SemaphoreType.DMA((64,)), pltpu.SemaphoreType.DMA((8,))],
        compiler_params=pltpu.CompilerParams(collective_id=0, has_side_effects=True, vmem_limit_bytes=40 * 2**20))(q, k, v, o)


def finish_kernel(part, out, RB, TB, TL, NB, send, recv, tsend, trecv, wsem):
    z, y, s = lax.axis_index("width"), lax.axis_index("row"), lax.axis_index("src")
    me = s * 4 + z
    at = {"width": z, "row": y, "src": s}
    partner = 3 - y
    barrier = pltpu.get_barrier_semaphore()

    def peer(d):
        n = (me + d) % 32
        return n, {"width": n % 4, "row": y, "src": n // 4}

    def greet(d, c):
        pl.semaphore_signal(barrier, inc=1, device_id=peer(d)[1], device_id_type=MESH)
        return c
    lax.fori_loop(1, 32, greet, 0)
    pl.semaphore_signal(barrier, inc=1, device_id={**at, "row": partner}, device_id_type=MESH)
    t = jnp.concatenate([jnp.sum(part[a].reshape(128, 8, 128), axis=0) for a in (0, 1)], axis=0)
    TL[...] = t
    TB[me] = t
    pl.semaphore_wait(barrier, 32)

    def block_to(d):
        n, where = peer(d)
        return pltpu.make_async_remote_copy(part.at[:, pl.ds(n * 32, 32), :], RB.at[me], send.at[d], recv.at[d], device_id=where, device_id_type=MESH)

    def total_to(d):
        n, where = peer(d)
        return pltpu.make_async_remote_copy(TL, TB.at[me], tsend.at[d], trecv.at[d], device_id=where, device_id_type=MESH)

    def begin(d, c):
        block_to(d).start()
        total_to(d).start()
        return c
    lax.fori_loop(1, 32, begin, 0)
    RB[me] = part[:, pl.ds(pl.multiple_of(me * 32, 32), 32), :]

    def finish(d, c):
        block_to(d).wait()
        total_to(d).wait()
        return c
    lax.fori_loop(1, 32, finish, 0)
    norms = jnp.sum(RB[...], axis=0)
    tb = jnp.sum(TB[...], axis=0)
    p = pair_of(y)
    share = []
    for a, ib in ((0, p), (1, 7 - p)):
        total = jnp.sum(tb[8 * a:8 * a + 8], axis=0, keepdims=True)
        pos = (ib * 128 + 1 + lax.broadcasted_iota(jnp.int32, (1, 128), 1)).astype(F32)
        share.append(jnp.transpose(norms[a] * (pos / total)))
    low = y < 2
    kept, other = jnp.where(low, share[0], share[1]), jnp.where(low, share[1], share[0])
    out[0:128, :] = kept
    NB[...] = other
    cp = pltpu.make_async_remote_copy(NB, out.at[pl.ds(128, 128), :], wsem.at[0], wsem.at[1], device_id={**at, "row": partner}, device_id_type=MESH)
    cp.start()
    cp.wait()


def finish(part):
    vm = pl.BlockSpec(memory_space=pltpu.VMEM)
    D = pltpu.SemaphoreType.DMA((32,))
    return pl.pallas_call(finish_kernel, out_shape=jax.ShapeDtypeStruct((256, 32), F32),
        in_specs=[vm], out_specs=vm,
        scratch_shapes=[pltpu.VMEM((32, 2, 32, 128), F32), pltpu.VMEM((32, 16, 128), F32), pltpu.VMEM((16, 128), F32), pltpu.VMEM((128, 32), F32),
                        D, D, D, D, pltpu.SemaphoreType.DMA((2,))],
        compiler_params=pltpu.CompilerParams(collective_id=1, has_side_effects=True))(part)


def body(query_rows, key_rows, value_rows, out_proj):
    q, k, v, o = gather(query_rows, key_rows, value_rows, out_proj)
    return finish(contributions(q, k, v, o))


def solution(mesh):
    placed = (PS_("row", "width"), PS_("src", "width"), PS_("src", None), PS_(("row", "src"), "width"))
    return jax.shard_map(
        body, mesh=mesh, in_specs=placed, out_specs=PS_("row", ("src", "width")), check_vma=False
    )
```

```python
import math
import jax, jax.numpy as jnp
from jax import lax
from jax.experimental import pallas as pl
from jax.experimental.pallas import tpu as pltpu
from jax.sharding import PartitionSpec as PS_
C2 = math.log2(math.e) / math.sqrt(128.0)
F32, BF = jnp.float32, jnp.bfloat16
NEG = -1e30
PS, IS = 17, 65

def pair_of(y):
    return jnp.where(y == 0, 0, jnp.where(y == 3, 1, y + 1))

SCR = [pltpu.VMEM((8, 128 * PS, 128), F32), pltpu.VMEM((9, 128, 64, 128), BF),
       pltpu.VMEM((8, 16, 128), F32), pltpu.VMEM((8, 16, 128), F32), pltpu.VMEM((8, 16, 128), F32),
       pltpu.VMEM((2, 128 * IS, 128), F32)]


MESH = pl.DeviceIdType.MESH


class Links:
    def __init__(self, send, recv, at=None):
        self.send, self.recv, self.n, self.at = send, recv, 0, at

    def to(self, source, target, **where):
        i = self.n
        self.n += 1
        return pltpu.make_async_remote_copy(src_ref=source, dst_ref=target, send_sem=self.send.at[i], recv_sem=self.recv.at[i],
                                            device_id={**self.at, **where}, device_id_type=MESH)


def layer_kernel(qi, ki, vi, oi, out, Q, K, V, OC, P, W, MS, LS, FS, IM, part, RB, TB, TL, NB,
                 send, recv, local, rsend, rrecv, tsend, trecv, wsem):
    z, y, s = lax.axis_index("width"), lax.axis_index("row"), lax.axis_index("src")
    x, c = s // 2, s % 2
    me = s * 4 + z
    p = pair_of(y)
    big = 7 - p
    at = {"width": z, "row": y, "src": s}
    zu, zd, zf = (z + 1) % 4, (z + 3) % 4, (z + 2) % 4
    yu, yd = (y + 1) % 4, (y + 3) % 4
    xu, xd, xf = (x + 1) % 4, (x + 3) % 4, (x + 2) % 4
    su, sd, sib = xu * 2 + c, xd * 2 + c, x * 2 + 1 - c
    partner = 3 - y
    tslot = y // 2

    barrier = pltpu.get_barrier_semaphore()

    def peer(n):
        return {"width": n % 4, "row": y, "src": n // 4}

    def greet(d, carry):
        pl.semaphore_signal(barrier, inc=1, device_id=peer((me + d) % 32), device_id_type=MESH)
        return carry
    lax.fori_loop(1, 32, greet, 0)
    for r in (yu, yd):
        pl.semaphore_signal(barrier, inc=1, device_id={**at, "row": r}, device_id_type=MESH)
    pl.semaphore_wait(barrier, 33)

    links = Links(send, recv, at)
    to = links.to
    mine = pl.ds(s * 128, 128)

    def rows(a):
        return pl.ds((a * 2 + c) * 128, 128)

    def oblock(a, b, ch):
        return OC.at[ch, pl.ds((a * 8 + b) * 256, 256), :]

    def orows(ch, a, lo, n):
        return OC.at[ch, pl.ds(a * 2048 + lo, n), :]

    def both(ref, *wheres):
        return [to(ref, ref, **w) for w in wheres]

    ups = [dict(src=su), dict(src=sd), dict(src=sib)]
    swap = to(qi.at[pl.ds(128, 128), :], Q.at[z, c], row=partner)
    loc_q = pltpu.make_async_copy(qi.at[pl.ds(0, 128), :], Q.at[z, c], local.at[0])
    locs = [pltpu.make_async_copy(ki, K.at[z, mine, :], local.at[1]), pltpu.make_async_copy(vi, V.at[mine, :], local.at[2])]
    locs += [pltpu.make_async_copy(oi.at[:, pl.ds(s * 256 + ch * 128, 128)], oblock(y, s, ch), local.at[3 + ch]) for ch in (0, 1)]
    kz = [to(ki, K.at[z, mine, :], width=w) for w in (zu, zd)]
    ox = [[to(oi.at[:, pl.ds(((s + d) % 8) * 256 + ch * 128, 128)], oblock(y, s, ch), src=(s + d) % 8) for d in range(1, 8)] for ch in (0, 1)]
    vx = [to(vi, V.at[mine, :], **w) for w in ups]
    qz = both(Q.at[z, c], dict(width=zu), dict(width=zd))
    qs = [both(Q.at[a, c], dict(src=sib))[0] for a in (z, zd, zu, zf)]
    lo, hi = pl.ds(s * 128, 64), pl.ds(s * 128 + 64, 64)
    kf = both(K.at[zd, lo, :], dict(width=zu)) + both(K.at[zu, hi, :], dict(width=zd))
    kx = both(K.at[:, mine, :], *ups)
    kxf = both(K.at[pl.ds(0, 2), rows(xd), :], dict(src=su)) + both(K.at[pl.ds(2, 2), rows(xu), :], dict(src=sd))
    kg = [both(K.at[:, rows(a), :], dict(src=sib))[0] for a in (xd, xu, xf)]
    vf = both(V.at[pl.ds((xd * 2 + c) * 128, 64), :], dict(src=su)) + both(V.at[pl.ds((xu * 2 + c) * 128 + 64, 64), :], dict(src=sd))
    vg = [both(V.at[rows(a), :], dict(src=sib))[0] for a in (xd, xu, xf)]
    qf = both(Q.at[zd, c, pl.ds(0, 64)], dict(width=zu)) + both(Q.at[zu, c, pl.ds(64, 64)], dict(width=zd))
    oy = [both(orows(ch, y, 0, 2048), dict(row=yu), dict(row=yd)) for ch in (0, 1)]
    of = [both(orows(ch, yd, 0, 1024), dict(row=yu)) + both(orows(ch, yu, 1024, 1024), dict(row=yd)) for ch in (0, 1)]

    def start(*copies):
        for cp in copies:
            cp.start()

    def arrived(*copies):
        for cp in copies:
            cp.wait_recv()

    start(*locs, *kz)

    @pl.when(c == tslot)
    def _():
        loc_q.start()
        swap.start()
    start(*ox[0])

    @pl.when(c == tslot)
    def _():
        loc_q.wait()
        start(*qz, qs[0])
    arrived(kz[0])
    start(kf[0])
    arrived(kz[1])
    start(kf[1])
    for cp in locs:
        cp.wait()
    arrived(*kf)
    start(*kx)

    @pl.when(c != tslot)
    def _():
        arrived(swap)
        start(*qz, qs[0])
    arrived(kx[0])
    start(kxf[0], kg[0])
    arrived(kx[1])
    start(kxf[1], kg[1])
    arrived(*ox[0])
    start(*oy[0])
    start(*ox[1], *vx)
    arrived(*kxf)
    start(kg[2])
    part[...] = jnp.zeros(part.shape, F32)
    arrived(kx[2], *kg, qs[0])

    jl = lax.broadcasted_iota(jnp.int32, (128, 256), 0)
    il = lax.broadcasted_iota(jnp.int32, (128, 256), 1) % 128

    def scores(zc, slot, ib, base):
        MS[...] = jnp.full(MS.shape, NEG, F32)
        LS[...] = jnp.zeros(LS.shape, F32)

        def block(jb, diag):
            for hp in range(8):
                kk = K[zc, pl.ds(pl.multiple_of(jb * 128, 128), 128), (hp // 4) * 128:(hp // 4 + 1) * 128]
                qq = jnp.concatenate([Q[zc, slot, :, (2 * hp + a) * 128:(2 * hp + a + 1) * 128] for a in (0, 1)], axis=0)
                sc = lax.dot_general(kk, qq, (((1,), (1,)), ((), ())), preferred_element_type=F32)
                if diag:
                    sc = jnp.where(jl <= il, sc, NEG)
                m = jnp.max(sc, axis=0, keepdims=True)
                e = jnp.exp2((sc - m) * C2)
                l = jnp.sum(e, axis=0, keepdims=True)
                for a in (0, 1):
                    lanes = slice(a * 128, (a + 1) * 128)
                    P[jb, pl.ds(2 * hp + a, 128, stride=PS), :] = e[:, lanes]
                    MS[jb, 2 * hp + a:2 * hp + a + 1, :] = m[:, lanes]
                    LS[jb, 2 * hp + a:2 * hp + a + 1, :] = l[:, lanes]

        def plain(jb, carry):
            block(jb, False)
            return carry
        lax.fori_loop(0, ib, plain, 0)
        block(ib, True)
        ms = MS[...]
        f = jnp.exp2((ms - jnp.max(ms, axis=0, keepdims=True)) * C2)
        total = jnp.sum(f * LS[...], axis=0, keepdims=True)
        FS[...] = f / total

        def conv(jb, carry):
            fs = FS[jb]
            for j in range(128):
                W[base + jb, j, pl.ds(pl.multiple_of(zc * 16, 16), 16), :] = (P[jb, j * PS:j * PS + 16, :] * fs).astype(BF)
            return carry
        lax.fori_loop(0, ib + 1, conv, 0)

    def zstep(d, carry):
        @pl.when(d == 1)
        def _():
            arrived(*ox[1])
            start(*oy[1])
            arrived(qz[0])
            start(qf[0], qs[1])
            arrived(qz[1])
            start(qf[1], qs[2])
            arrived(vx[0])
            start(vf[0], vg[0])
            arrived(vx[1])
            start(vf[1], vg[1])
            arrived(qs[1])

        @pl.when(d == 2)
        def _():
            arrived(oy[0][0])
            start(of[0][0])
            arrived(oy[0][1])
            start(of[0][1])
            arrived(*vf)
            start(vg[2])
            arrived(*qf)
            start(qs[3])
            arrived(qs[2])

        @pl.when(d == 3)
        def _():
            arrived(qs[3])
        zc = (z + jnp.where(d == 1, 3, jnp.where(d == 2, 1, jnp.where(d == 3, 2, 0)))) % 4
        scores(zc, 0, p, big + 1)
        scores(zc, 1, big, 0)
        return carry
    lax.fori_loop(0, 4, zstep, 0)

    arrived(oy[1][0])
    start(of[1][0])
    arrived(oy[1][1])
    start(of[1][1])
    arrived(vx[2], *vg, *of[0], *of[1])

    def block_to(n):
        return pltpu.make_async_remote_copy(part.at[:, pl.ds(n * 32, 32), :], RB.at[me], rsend.at[n], rrecv.at[me], device_id=peer(n), device_id_type=MESH)

    def block_from(n):
        return pltpu.make_async_remote_copy(part.at[:, pl.ds(n * 32, 32), :], RB.at[n], rsend.at[n], rrecv.at[n], device_id=peer(n), device_id_type=MESH)

    def total_to(d):
        return pltpu.make_async_remote_copy(TL, TB.at[me], tsend.at[d], trecv.at[d], device_id=peer((me + d) % 32), device_id_type=MESH)

    def jstep(jb, carry):
        def img(g, carry):
            vvs = [V[pl.ds(pl.multiple_of(jb * 128, 128), 128), pl.ds(pl.multiple_of(g * 256 + b * 128, 128), 128)] for b in (0, 1)]
            for hh in range(16):
                h = g * 16 + hh
                oo = jnp.concatenate([OC[a, pl.ds(pl.multiple_of(h * 128, 128), 128), :] for a in (0, 1)], axis=1)
                im = jnp.dot(vvs[hh // 8], oo, preferred_element_type=F32)
                for a in (0, 1):
                    IM[a, pl.ds(h, 128, stride=IS), :] = im[:, a * 128:(a + 1) * 128]
            return carry
        lax.fori_loop(0, 4, img, 0)

        def contrib(t, slot):
            zero = jnp.zeros((64, 128), BF)
            PU = 32

            def pairs(n, carry):
                got = []
                for u in range(PU):
                    j = n * (2 * PU) + 2 * u
                    r0 = pl.multiple_of(n * (2 * PU * IS), 8)
                    lhs = jnp.concatenate([jnp.concatenate([IM[a, pl.ds(r0 + (2 * u + b) * IS, 64), :].astype(BF) for b in (0, 1)], axis=0) for a in (0, 1)], axis=1)
                    rhs = jnp.concatenate([
                        jnp.concatenate([W[t, j], zero], axis=1),
                        jnp.concatenate([zero, W[t, j + 1]], axis=1)], axis=0)
                    cc = lax.dot_general(lhs, rhs, (((0,), (0,)), ((), ())), preferred_element_type=F32)
                    r = jnp.sum(jnp.abs(cc), axis=0, keepdims=True)
                    got += [r[:, :128], r[:, 128:]]
                for b in range(PU // 4):
                    part[slot, pl.ds(pl.multiple_of(jb * 128 + n * (2 * PU) + 8 * b, 8), 8), :] = jnp.concatenate(got[8 * b:8 * b + 8], axis=0)
                return carry
            lax.fori_loop(0, 128 // (2 * PU), pairs, 0)
        contrib(jb, 1)

        @pl.when(jb <= p)
        def _():
            contrib(big + 1 + jb, 0)
        for w in range(4):
            n = jb * 4 + w

            @pl.when(n != me)
            def _():
                block_to(n).start()
        return carry
    lax.fori_loop(0, big + 1, jstep, 0)

    tl = jnp.concatenate([jnp.sum(part[a].reshape(128, 8, 128), axis=0) for a in (0, 1)], axis=0)
    TL[...] = tl
    TB[me] = tl

    def tell(d, carry):
        total_to(d).start()
        return carry
    lax.fori_loop(1, 32, tell, 0)
    RB[me] = part[:, pl.ds(pl.multiple_of(me * 32, 32), 32), :]

    def heard(d, carry):
        total_to(d).wait()
        return carry
    lax.fori_loop(1, 32, heard, 0)
    for cp in kz + ox[0] + ox[1] + vx + qz + qs + kf + kx + vf + vg + kxf + kg + qf + oy[0] + oy[1] + of[0] + of[1]:
        cp.wait_send()

    @pl.when(c == tslot)
    def _():
        swap.wait_send()

    def sent(n, carry):
        @pl.when(n != me)
        def _():
            block_to(n).wait_send()
        return carry
    lax.fori_loop(0, (big + 1) * 4, sent, 0)

    tb = jnp.sum(TB[...], axis=0)

    def scale(a, ib):
        total = jnp.sum(tb[8 * a:8 * a + 8], axis=0, keepdims=True)
        pos = (ib * 128 + 1 + lax.broadcasted_iota(jnp.int32, (1, 128), 1)).astype(F32)
        return pos / total

    def emit(first, second):
        low = y < 2
        out[:, 0:128] = jnp.where(low, first, second)
        NB[...] = jnp.where(low, second, first)

    @pl.when(s <= big)
    def _():
        def take(n, carry):
            @pl.when(n != me)
            def _():
                block_from(n).wait_recv()
            return carry
        lax.fori_loop(0, 32, take, 0)
        norms = jnp.sum(RB[...], axis=0)
        emit(norms[0] * scale(0, p), norms[1] * scale(1, big))

    @pl.when(s > big)
    def _():
        emit(jnp.zeros((32, 128), F32), jnp.zeros((32, 128), F32))
    back = pltpu.make_async_remote_copy(NB, out.at[:, pl.ds(128, 128)], wsem.at[0], wsem.at[1], device_id={**at, "row": partner}, device_id_type=MESH)
    back.start()
    back.wait()


def body(query_rows, key_rows, value_rows, out_proj):
    hbm = pl.BlockSpec(memory_space=pl.ANY)
    D = pltpu.SemaphoreType.DMA
    out = pl.pallas_call(
        layer_kernel, out_shape=jax.ShapeDtypeStruct((32, 256), F32), in_specs=[hbm] * 4,
        out_specs=pl.BlockSpec(memory_space=pltpu.VMEM),
        scratch_shapes=[
            pltpu.VMEM((4, 2, 128, 2048), BF), pltpu.VMEM((4, 1024, 256), BF), pltpu.VMEM((1024, 1024), BF), pltpu.VMEM((2, 8192, 128), BF),
            *SCR, pltpu.VMEM((2, 1024, 128), F32), pltpu.VMEM((32, 2, 32, 128), F32), pltpu.VMEM((32, 16, 128), F32),
            pltpu.VMEM((16, 128), F32), pltpu.VMEM((32, 128), F32),
            D((64,)), D((64,)), D((8,)), D((32,)), D((32,)), D((32,)), D((32,)), D((2,))],
        compiler_params=pltpu.CompilerParams(collective_id=0, has_side_effects=True, vmem_limit_bytes=62 * 2**20),
    )(query_rows, key_rows, value_rows, out_proj)
    return out.T


def solution(mesh):
    placed = (PS_("row", "width"), PS_("src", "width"), PS_("src", None), PS_(("row", "src"), "width"))
    return jax.shard_map(
        body, mesh=mesh, in_specs=placed, out_specs=PS_("row", ("src", "width")), check_vma=False
    )
```

```python
import math
import jax, jax.numpy as jnp
from jax import lax
from jax.experimental import pallas as pl
from jax.experimental.pallas import tpu as pltpu
from jax.sharding import PartitionSpec as PS_
C2 = math.log2(math.e) / math.sqrt(128.0)
F32, BF = jnp.float32, jnp.bfloat16
NEG = -1e30
PS, IS = 17, 65

SCR = [pltpu.VMEM((8, 128 * PS, 128), F32), pltpu.VMEM((9, 128, 64, 128), BF),
       pltpu.VMEM((8, 16, 128), F32), pltpu.VMEM((8, 16, 128), F32), pltpu.VMEM((8, 16, 128), F32),
       pltpu.VMEM((2, 128 * IS, 128), F32)]


MESH = pl.DeviceIdType.MESH


class Links:
    def __init__(self, send, recv, at=None):
        self.send, self.recv, self.n, self.at = send, recv, 0, at

    def to(self, source, target, **where):
        i = self.n
        self.n += 1
        return pltpu.make_async_remote_copy(src_ref=source, dst_ref=target, send_sem=self.send.at[i], recv_sem=self.recv.at[i],
                                            device_id={**self.at, **where}, device_id_type=MESH)


def layer_kernel(qi, ki, vi, oi, out, Q, K, V, OC, P, W, MS, LS, FS, IM, part, RB, TB, TL, NB,
                 send, recv, local, rsend, rrecv, tsend, trecv, wsend, wrecv):
    z, y, s = lax.axis_index("width"), lax.axis_index("row"), lax.axis_index("src")
    x, c = s // 2, s % 2
    me = s * 4 + z
    p = (x + y) % 4
    big = 7 - p
    at = {"width": z, "row": y, "src": s}
    zu, zd, zf = (z + 1) % 4, (z + 3) % 4, (z + 2) % 4
    yu, yd = (y + 1) % 4, (y + 3) % 4
    xu, xd = (x + 1) % 4, (x + 3) % 4
    su, sd, sib = xu * 2 + c, xd * 2 + c, x * 2 + 1 - c

    barrier = pltpu.get_barrier_semaphore()

    def peer(n):
        return {"width": n % 4, "row": (p + 4 - n // 8) % 4, "src": n // 4}

    def greet(**where):
        pl.semaphore_signal(barrier, inc=1, device_id={**at, **where}, device_id_type=MESH)

    def greet_peer(d, carry):
        greet(**peer((me + d) % 32))
        return carry
    for d in range(1, 8):
        greet(src=(s + d) % 8)
    for d in range(1, 4):
        for b in (0, 1):
            greet(row=(y + d) % 4, src=x * 2 + b)
    lax.fori_loop(1, 32, greet_peer, 0)
    pl.semaphore_wait(barrier, 44)

    links = Links(send, recv, at)
    to = links.to

    def both(ref, *wheres):
        return [to(ref, ref, **w) for w in wheres]

    rows = y * 2 + c
    pair = jnp.where(rows < 4, rows, 7 - rows)
    goal, slot_to = (pair + 4 - x) % 4, y // 2
    stays = jnp.logical_and(goal == y, slot_to == c)
    q_half = qi.at[pl.ds(c * 128, 128), :]
    move = to(q_half, Q.at[z, slot_to], row=goal, src=x * 2 + slot_to)
    keep = pltpu.make_async_copy(q_half, Q.at[z, c], local.at[0])
    v_own = vi.at[:, pl.ds(z * 256, 256)]

    def o_src(b):
        return oi.at[:, pl.ds(b * 128, 128)]

    def o_dst(ch):
        return OC.at[ch, y, pl.ds(s * 256, 256), :]
    loc_k = pltpu.make_async_copy(ki, K.at[z, x, c], local.at[1])
    loc_v = pltpu.make_async_copy(v_own, V.at[z, x, c], local.at[2])
    loc_o = [pltpu.make_async_copy(o_src(s), o_dst(0), local.at[3]), pltpu.make_async_copy(o_src(8 + y * 2 + c), o_dst(1), local.at[4])]
    kx = [to(ki, K.at[z, x, c], src=(s + d) % 8) for d in range(1, 8)]
    vx = [to(v_own, V.at[z, x, c], src=(s + d) % 8) for d in range(1, 8)]
    oa = [to(o_src((s + d) % 8), o_dst(0), src=(s + d) % 8) for d in range(1, 8)]
    ob = [to(o_src(8 + ((y + d) % 4) * 2 + (c + b) % 2), o_dst(1), row=(y + d) % 4, src=x * 2 + (c + b) % 2) for d in range(1, 4) for b in (0, 1)]
    ob += [to(o_src(8 + y * 2 + 1 - c), o_dst(1), src=sib)]
    ups, downs, other = dict(width=zu), dict(width=zd), dict(src=sib)
    kz = both(K.at[z, :, c], ups, downs)
    vz = both(V.at[z, :, c], ups, downs)
    qz = both(Q.at[z, c], ups, downs)
    kf = both(K.at[zd, pl.ds(0, 2), c], ups) + both(K.at[zu, pl.ds(2, 2), c], downs)
    vf = both(V.at[zd, pl.ds(0, 2), c], ups) + both(V.at[zu, pl.ds(2, 2), c], downs)
    qf = both(Q.at[zd, c, pl.ds(0, 64)], ups) + both(Q.at[zu, c, pl.ds(64, 64)], downs)
    kg = [both(K.at[a, :, c], other)[0] for a in (zd, zu, zf)]
    vg = [both(V.at[a, :, c], other)[0] for a in (zd, zu, zf)]
    qs = [both(Q.at[a, c], other)[0] for a in (z, zd, zu, zf)]
    oy = both(OC.at[0, y], dict(row=yu), dict(row=yd))
    oyf = both(OC.at[0, yd, pl.ds(0, 1024)], dict(row=yu)) + both(OC.at[0, yu, pl.ds(1024, 1024)], dict(row=yd))
    ow = both(OC.at[1, :, pl.ds(x * 512, 512)], dict(src=su), dict(src=sd))
    owf = both(OC.at[1, pl.ds(0, 2), pl.ds(xd * 512, 512)], dict(src=su)) + both(OC.at[1, pl.ds(2, 2), pl.ds(xu * 512, 512)], dict(src=sd))
    remote = kx + vx + oa + ob + kz + vz + qz + kf + vf + qf + kg + vg + qs + oy + oyf + ow + owf

    def start(*copies):
        for cp in copies:
            cp.start()

    def arrived(*copies):
        for cp in copies:
            cp.wait_recv()

    start(loc_k, *kx)

    @pl.when(stays)
    def _():
        keep.start()

    @pl.when(jnp.logical_not(stays))
    def _():
        move.start()
    start(*loc_o, loc_v, *oa, *ob)
    loc_k.wait()
    arrived(*kx)
    start(*kz)

    @pl.when(stays)
    def _():
        keep.wait()

    @pl.when(jnp.logical_not(stays))
    def _():
        arrived(move)
    start(qs[0], *qz, *vx)
    for cp in loc_o:
        cp.wait()
    loc_v.wait()
    part[...] = jnp.zeros(part.shape, F32)
    arrived(*oa)
    start(*oy)
    arrived(*ob)
    start(*ow)
    arrived(qs[0])

    jl = lax.broadcasted_iota(jnp.int32, (128, 256), 0)
    il = lax.broadcasted_iota(jnp.int32, (128, 256), 1) % 128

    def scores(zc, slot, ib, base):
        MS[...] = jnp.full(MS.shape, NEG, F32)
        LS[...] = jnp.zeros(LS.shape, F32)

        def block(jb, diag):
            for hp in range(8):
                kk = K[zc, jb // 2, jb % 2, :, (hp // 4) * 128:(hp // 4 + 1) * 128]
                qq = jnp.concatenate([Q[zc, slot, :, (2 * hp + a) * 128:(2 * hp + a + 1) * 128] for a in (0, 1)], axis=0)
                sc = lax.dot_general(kk, qq, (((1,), (1,)), ((), ())), preferred_element_type=F32)
                if diag:
                    sc = jnp.where(jl <= il, sc, NEG)
                m = jnp.max(sc, axis=0, keepdims=True)
                e = jnp.exp2((sc - m) * C2)
                l = jnp.sum(e, axis=0, keepdims=True)
                for a in (0, 1):
                    lanes = slice(a * 128, (a + 1) * 128)
                    P[jb, pl.ds(2 * hp + a, 128, stride=PS), :] = e[:, lanes]
                    MS[jb, 2 * hp + a:2 * hp + a + 1, :] = m[:, lanes]
                    LS[jb, 2 * hp + a:2 * hp + a + 1, :] = l[:, lanes]

        def plain(jb, carry):
            block(jb, False)
            return carry
        lax.fori_loop(0, ib, plain, 0)
        block(ib, True)
        ms = MS[...]
        f = jnp.exp2((ms - jnp.max(ms, axis=0, keepdims=True)) * C2)
        total = jnp.sum(f * LS[...], axis=0, keepdims=True)
        FS[...] = f / total

        def conv(jb, carry):
            fs = FS[jb]
            for j in range(128):
                W[base + jb, j, pl.ds(pl.multiple_of(zc * 16, 16), 16), :] = (P[jb, j * PS:j * PS + 16, :] * fs).astype(BF)
            return carry
        lax.fori_loop(0, ib + 1, conv, 0)

    def zstep(d, carry):
        @pl.when(d == 1)
        def _():
            arrived(*vx)
            start(*vz)
            for h in (0, 1):
                arrived(kz[h])
                start(kf[h], kg[h])
            for h in (0, 1):
                arrived(qz[h])
                start(qf[h], qs[1 + h])
            arrived(kg[0], qs[1])

        @pl.when(d == 2)
        def _():
            for h in (0, 1):
                arrived(oy[h])
                start(oyf[h])
            for h in (0, 1):
                arrived(ow[h])
                start(owf[h])
            for h in (0, 1):
                arrived(vz[h])
                start(vf[h], vg[h])
            arrived(kg[1], qs[2])

        @pl.when(d == 3)
        def _():
            arrived(*kf)
            start(kg[2])
            arrived(*qf)
            start(qs[3])
            arrived(kg[2], qs[3])
        zc = (z + jnp.where(d == 1, 3, jnp.where(d == 2, 1, jnp.where(d == 3, 2, 0)))) % 4
        scores(zc, 0, p, big + 1)
        scores(zc, 1, big, 0)
        return carry
    lax.fori_loop(0, 4, zstep, 0)

    arrived(*vf)
    start(vg[2])
    arrived(*vg, *oyf, *owf)

    def block_to(n):
        return pltpu.make_async_remote_copy(part.at[:, pl.ds(n * 32, 32), :], RB.at[me], rsend.at[n], rrecv.at[me], device_id=peer(n), device_id_type=MESH)

    def block_from(n):
        return pltpu.make_async_remote_copy(part.at[:, pl.ds(n * 32, 32), :], RB.at[n], rsend.at[n], rrecv.at[n], device_id=peer(n), device_id_type=MESH)

    def total_to(d):
        return pltpu.make_async_remote_copy(TL, TB.at[me], tsend.at[d], trecv.at[d], device_id=peer((me + d) % 32), device_id_type=MESH)

    turn = (x * (big + 1)) // 4

    def jstep(t, carry):
        jb = jnp.where(t + turn > big, t + turn - big - 1, t + turn)
        for h in range(64):
            vv = V[h // 16, jb // 2, jb % 2, :, (h // 8 % 2) * 128:(h // 8 % 2 + 1) * 128]
            oo = jnp.concatenate([OC[a, h // 16, (h % 16) * 128:(h % 16 + 1) * 128, :] for a in (0, 1)], axis=1)
            im = jnp.dot(vv, oo, preferred_element_type=F32)
            for a in (0, 1):
                IM[a, pl.ds(h, 128, stride=IS), :] = im[:, a * 128:(a + 1) * 128]

        def contrib(t, slot):
            zero = jnp.zeros((64, 128), BF)
            PU = 64

            def pairs(n, carry):
                got = []
                for u in range(PU):
                    j = n * (2 * PU) + 2 * u
                    r0 = pl.multiple_of(n * (2 * PU * IS), 8)
                    lhs = jnp.concatenate([jnp.concatenate([IM[a, pl.ds(r0 + (2 * u + b) * IS, 64), :].astype(BF) for b in (0, 1)], axis=0) for a in (0, 1)], axis=1)
                    rhs = jnp.concatenate([
                        jnp.concatenate([W[t, j], zero], axis=1),
                        jnp.concatenate([zero, W[t, j + 1]], axis=1)], axis=0)
                    cc = lax.dot_general(lhs, rhs, (((0,), (0,)), ((), ())), preferred_element_type=F32)
                    r = jnp.sum(jnp.abs(cc), axis=0, keepdims=True)
                    got += [r[:, :128], r[:, 128:]]
                for b in range(PU // 4):
                    part[slot, pl.ds(pl.multiple_of(jb * 128 + n * (2 * PU) + 8 * b, 8), 8), :] = jnp.concatenate(got[8 * b:8 * b + 8], axis=0)
                return carry
            lax.fori_loop(0, 128 // (2 * PU), pairs, 0)
        contrib(jb, 1)

        @pl.when(jb <= p)
        def _():
            contrib(big + 1 + jb, 0)
        for w in range(4):
            n = jb * 4 + w

            @pl.when(n != me)
            def _():
                block_to(n).start()
        return carry
    lax.fori_loop(0, big + 1, jstep, 0)

    tl = jnp.concatenate([jnp.sum(part[a].reshape(128, 8, 128), axis=0) for a in (0, 1)], axis=0)
    TL[...] = tl
    TB[me] = tl

    def tell(d, carry):
        total_to(d).start()
        return carry
    lax.fori_loop(1, 32, tell, 0)
    RB[me] = part[:, pl.ds(pl.multiple_of(me * 32, 32), 32), :]

    def heard(d, carry):
        total_to(d).wait()
        return carry
    lax.fori_loop(1, 32, heard, 0)
    for cp in remote:
        cp.wait_send()

    @pl.when(jnp.logical_not(stays))
    def _():
        move.wait_send()

    def sent(n, carry):
        @pl.when(n != me)
        def _():
            block_to(n).wait_send()
        return carry
    lax.fori_loop(0, (big + 1) * 4, sent, 0)

    tb = jnp.sum(TB[...], axis=0)

    def scale(a, ib):
        total = jnp.sum(tb[8 * a:8 * a + 8], axis=0, keepdims=True)
        pos = (ib * 128 + 1 + lax.broadcasted_iota(jnp.int32, (1, 128), 1)).astype(F32)
        return pos / total

    def emit(first, second):
        NB[0] = first
        NB[1] = second

    @pl.when(s <= big)
    def _():
        def take(n, carry):
            @pl.when(n != me)
            def _():
                block_from(n).wait_recv()
            return carry
        lax.fori_loop(0, 32, take, 0)
        norms = jnp.sum(RB[...], axis=0)
        emit(norms[0] * scale(0, p), norms[1] * scale(1, big))

    @pl.when(s > big)
    def _():
        emit(jnp.zeros((32, 128), F32), jnp.zeros((32, 128), F32))

    def home(a):
        ib = (p, big)[a]
        return ib // 2, ib % 2, pltpu.make_async_remote_copy(NB.at[a], out.at[ib % 2], wsend.at[a], wrecv.at[ib % 2], device_id={**at, "row": ib // 2}, device_id_type=MESH)

    for a in (0, 1):
        owner, half, cp = home(a)

        @pl.when(owner == y)
        def _():
            out[half] = NB[a]

        @pl.when(owner != y)
        def _():
            cp.start()
    for h in (0, 1):
        ib = y * 2 + h
        came = (jnp.where(ib < 4, ib, 7 - ib) + 4 - x) % 4

        @pl.when(came != y)
        def _():
            pltpu.make_async_remote_copy(NB.at[h], out.at[h], wsend.at[h], wrecv.at[h], device_id={**at, "row": came}, device_id_type=MESH).wait_recv()
    for a in (0, 1):
        owner, half, cp = home(a)

        @pl.when(owner != y)
        def _():
            cp.wait_send()


def body(query_rows, key_rows, value_rows, out_proj):
    hbm = pl.BlockSpec(memory_space=pl.ANY)
    D = pltpu.SemaphoreType.DMA
    out = pl.pallas_call(
        layer_kernel, out_shape=jax.ShapeDtypeStruct((2, 32, 128), F32), in_specs=[hbm] * 4,
        out_specs=pl.BlockSpec(memory_space=pltpu.VMEM),
        scratch_shapes=[
            pltpu.VMEM((4, 2, 128, 2048), BF), pltpu.VMEM((4, 4, 2, 128, 256), BF), pltpu.VMEM((4, 4, 2, 128, 256), BF), pltpu.VMEM((2, 4, 2048, 128), BF),
            *SCR, pltpu.VMEM((2, 1024, 128), F32), pltpu.VMEM((32, 2, 32, 128), F32), pltpu.VMEM((32, 16, 128), F32),
            pltpu.VMEM((16, 128), F32), pltpu.VMEM((2, 32, 128), F32),
            D((80,)), D((80,)), D((8,)), D((32,)), D((32,)), D((32,)), D((32,)), D((2,)), D((2,))],
        compiler_params=pltpu.CompilerParams(collective_id=0, has_side_effects=True, vmem_limit_bytes=62 * 2**20),
    )(query_rows, key_rows, value_rows, out_proj)
    return out.transpose(0, 2, 1).reshape(256, 32)


def solution(mesh):
    placed = (PS_("row", "width"), PS_("src", "width"), PS_("src", None), PS_(("row", "src"), "width"))
    return jax.shard_map(
        body, mesh=mesh, in_specs=placed, out_specs=PS_("row", ("src", "width")), check_vma=False
    )
```

```python
import math
import jax, jax.numpy as jnp
from jax import lax
from jax.experimental import pallas as pl
from jax.experimental.pallas import tpu as pltpu
from jax.sharding import PartitionSpec as PS_
C2 = math.log2(math.e) / math.sqrt(128.0)
F32, BF = jnp.float32, jnp.bfloat16
NEG = -1e30
PS, IS = 17, 65

SCR = [pltpu.VMEM((8, 128 * PS, 128), F32), pltpu.VMEM((9, 128, 64, 128), BF),
       pltpu.VMEM((8, 16, 128), F32), pltpu.VMEM((8, 16, 128), F32), pltpu.VMEM((8, 16, 128), F32),
       pltpu.VMEM((2, 128 * IS, 128), F32)]


MESH = pl.DeviceIdType.MESH


def mixed(a, b):
    return (a // 2 + b // 2) % 2 * 2 + (a + b) % 2


class Links:
    def __init__(self, send, recv, at=None):
        self.send, self.recv, self.n, self.at = send, recv, 0, at

    def to(self, source, target, **where):
        i = self.n
        self.n += 1
        return pltpu.make_async_remote_copy(src_ref=source, dst_ref=target, send_sem=self.send.at[i], recv_sem=self.recv.at[i],
                                            device_id={**self.at, **where}, device_id_type=MESH)


def layer_kernel(qi, ki, vi, oi, out, Q, K, V, OC, P, W, MS, LS, FS, IM, part, RB, TB, TL, NB,
                 send, recv, local, rsend, rrecv, tsend, trecv, wsend, wrecv, ready):
    z, y, s = lax.axis_index("width"), lax.axis_index("row"), lax.axis_index("src")
    x, c = s // 2, s % 2
    me = s * 4 + z
    p = mixed(x, y)
    big = 7 - p
    at = {"width": z, "row": y, "src": s}
    zu, zd, zf = (z + 1) % 4, (z + 3) % 4, (z + 2) % 4
    yu, yd = (y + 1) % 4, (y + 3) % 4
    xu, xd, xf = (x + 1) % 4, (x + 3) % 4, (x + 2) % 4
    su, sd, sib = xu * 2 + c, xd * 2 + c, x * 2 + 1 - c

    barrier = pltpu.get_barrier_semaphore()

    def peer(n):
        return {"width": n % 4, "row": mixed(p, n // 8), "src": n // 4}

    def greet(**where):
        pl.semaphore_signal(barrier, inc=1, device_id={**at, **where}, device_id_type=MESH)

    for d in range(1, 8):
        greet(src=(s + d) % 8)
    for d in range(1, 4):
        for b in (0, 1):
            greet(row=(y + d) % 4, src=x * 2 + b)
    for w in (zu, zd, zf):
        greet(width=w)
    pl.semaphore_wait(barrier, 16)

    links = Links(send, recv, at)
    to = links.to

    def both(ref, *wheres):
        return [to(ref, ref, **w) for w in wheres]

    rows = y * 2 + c
    pair = jnp.where(rows < 4, rows, 7 - rows)
    goal, slot_to = mixed(pair, x), y // 2
    stays = jnp.logical_and(goal == y, slot_to == c)
    q_half = qi.at[pl.ds(c * 128, 128), :]
    move = [to(q_half.at[pl.ds(h * 64, 64), :], Q.at[z, slot_to, pl.ds(h * 64, 64)], row=goal, src=x * 2 + slot_to) for h in (0, 1)]
    keep = pltpu.make_async_copy(q_half, Q.at[z, c], local.at[0])

    def o_src(b):
        return oi.at[:, pl.ds(b * 128, 128)]

    def o_dst(ch):
        return OC.at[ch, y, pl.ds(s * 256, 256), :]
    loc_k = pltpu.make_async_copy(ki, K.at[z, x, c], local.at[1])
    loc_v = pltpu.make_async_copy(vi, V.at[x, c], local.at[2])
    loc_o = [pltpu.make_async_copy(o_src(s), o_dst(0), local.at[3]), pltpu.make_async_copy(o_src(8 + y * 2 + c), o_dst(1), local.at[4])]
    kx = [to(ki, K.at[z, x, c], src=(s + d) % 8) for d in (2, 4, 6)]
    vx = [to(vi, V.at[x, c], src=w) for w in (su, sd, sib)]
    oa = [to(o_src((s + d) % 8), o_dst(0), src=(s + d) % 8) for d in range(1, 8)]
    ob = [to(o_src(8 + ((y + d) % 4) * 2 + (c + b) % 2), o_dst(1), row=(y + d) % 4, src=x * 2 + (c + b) % 2) for d in range(1, 4) for b in (0, 1)]
    ob += [to(o_src(8 + y * 2 + 1 - c), o_dst(1), src=sib)]
    ups, downs, other = dict(width=zu), dict(width=zd), dict(src=sib)
    kz = both(K.at[z, :, c], ups, downs)
    qz = [both(Q.at[z, c, pl.ds(h * 64, 64)], ups, downs) for h in (0, 1)]
    kf = both(K.at[zd, pl.ds(0, 2), c], ups) + both(K.at[zu, pl.ds(2, 2), c], downs)
    vf = both(V.at[xd, c, pl.ds(0, 64)], dict(src=su)) + both(V.at[xu, c, pl.ds(64, 64)], dict(src=sd))
    qf = both(Q.at[zd, c, pl.ds(0, 64)], ups) + both(Q.at[zu, c, pl.ds(64, 64)], downs)
    kg = [both(K.at[a, :, c], other)[0] for a in (z, zd, zu, zf)]
    vg = [both(V.at[a, c], other)[0] for a in (xd, xu, xf)]
    qs = [both(Q.at[a, c], other)[0] for a in (z, zd, zu, zf)]
    oy = both(OC.at[0, y], dict(row=yu), dict(row=yd))
    oyf = both(OC.at[0, yd, pl.ds(0, 1024)], dict(row=yu)) + both(OC.at[0, yu, pl.ds(1024, 1024)], dict(row=yd))
    ow = both(OC.at[1, :, pl.ds(x * 512, 512)], dict(src=su), dict(src=sd))
    owf = both(OC.at[1, pl.ds(0, 2), pl.ds(xd * 512, 512)], dict(src=su)) + both(OC.at[1, pl.ds(2, 2), pl.ds(xu * 512, 512)], dict(src=sd))
    remote = kx + vx + oa + ob + kz + qz[0] + qz[1] + kf + vf + qf + kg + vg + qs + oy + oyf + ow + owf

    def start(*copies):
        for cp in copies:
            cp.start()

    def arrived(*copies):
        for cp in copies:
            cp.wait_recv()

    start(loc_k, *kx)

    @pl.when(stays)
    def _():
        keep.start()

    @pl.when(jnp.logical_not(stays))
    def _():
        start(*move)
    start(*loc_o, loc_v, *oa)
    loc_k.wait()
    arrived(*kx)
    start(*kz, kg[0])
    start(*ob, *vx)

    @pl.when(stays)
    def _():
        keep.wait()

    for h in (0, 1):
        @pl.when(jnp.logical_not(stays))
        def _():
            arrived(move[h])
        start(*qz[h])
    start(qs[0])
    for cp in loc_o:
        cp.wait()
    loc_v.wait()
    part[...] = jnp.zeros(part.shape, F32)
    arrived(*oa)
    start(*oy)
    arrived(*ob)
    start(*ow)
    for h in (0, 1):
        arrived(kz[h])
        start(kf[h], kg[1 + h])
    for h in (0, 1):
        arrived(vx[h])
        start(vf[h], vg[h])
    arrived(qz[0][0])
    start(qf[0])
    arrived(kg[0], qs[0])

    jl = lax.broadcasted_iota(jnp.int32, (128, 256), 0)
    il = lax.broadcasted_iota(jnp.int32, (128, 256), 1) % 128

    def scores(zc, slot, ib, base):
        MS[...] = jnp.full(MS.shape, NEG, F32)
        LS[...] = jnp.zeros(LS.shape, F32)

        def block(jb, diag):
            for hp in range(8):
                kk = K[zc, jb // 2, jb % 2, :, (hp // 4) * 128:(hp // 4 + 1) * 128]
                qq = jnp.concatenate([Q[zc, slot, :, (2 * hp + a) * 128:(2 * hp + a + 1) * 128] for a in (0, 1)], axis=0)
                sc = lax.dot_general(kk, qq, (((1,), (1,)), ((), ())), preferred_element_type=F32)
                if diag:
                    sc = jnp.where(jl <= il, sc, NEG)
                m = jnp.max(sc, axis=0, keepdims=True)
                e = jnp.exp2((sc - m) * C2)
                l = jnp.sum(e, axis=0, keepdims=True)
                for a in (0, 1):
                    lanes = slice(a * 128, (a + 1) * 128)
                    P[jb, pl.ds(2 * hp + a, 128, stride=PS), :] = e[:, lanes]
                    MS[jb, 2 * hp + a:2 * hp + a + 1, :] = m[:, lanes]
                    LS[jb, 2 * hp + a:2 * hp + a + 1, :] = l[:, lanes]

        def plain(jb, carry):
            block(jb, False)
            return carry
        lax.fori_loop(0, ib, plain, 0)
        block(ib, True)
        ms = MS[...]
        f = jnp.exp2((ms - jnp.max(ms, axis=0, keepdims=True)) * C2)
        total = jnp.sum(f * LS[...], axis=0, keepdims=True)
        FS[...] = f / total

        def conv(jb, carry):
            fs = FS[jb]
            for j in range(128):
                W[base + jb, j, pl.ds(pl.multiple_of(zc * 16, 16), 16), :] = (P[jb, j * PS:j * PS + 16, :] * fs).astype(BF)
            return carry
        lax.fori_loop(0, ib + 1, conv, 0)

    def zstep(d, carry):
        @pl.when(d == 1)
        def _():
            arrived(qz[0][1], qz[1][1])
            start(qf[1], qs[2])
            arrived(qz[1][0])
            start(qs[1])
            for h in (0, 1):
                arrived(oy[h])
                start(oyf[h])
            for h in (0, 1):
                arrived(ow[h])
                start(owf[h])
            arrived(kg[1], qs[1])

        @pl.when(d == 2)
        def _():
            arrived(*kf)
            start(kg[3])
            arrived(*vf)
            start(vg[2])
            arrived(kg[2], qs[2])

        @pl.when(d == 3)
        def _():
            arrived(*qf)
            start(qs[3])
            arrived(kg[3], qs[3])
        zc = (z + jnp.where(d == 1, 3, jnp.where(d == 2, 1, jnp.where(d == 3, 2, 0)))) % 4
        scores(zc, 0, p, big + 1)
        scores(zc, 1, big, 0)
        return carry
    lax.fori_loop(0, 4, zstep, 0)

    arrived(vx[2], *vg, *oyf, *owf)
    for w in (zu, zd, zf):
        pl.semaphore_signal(ready, inc=1, device_id={**at, "width": w}, device_id_type=MESH)

    def block_to(n):
        return pltpu.make_async_remote_copy(part.at[:, pl.ds(n * 32, 32), :], RB.at[me], rsend.at[n], rrecv.at[me], device_id=peer(n), device_id_type=MESH)

    def block_from(n):
        return pltpu.make_async_remote_copy(part.at[:, pl.ds(n * 32, 32), :], RB.at[n], rsend.at[n], rrecv.at[n], device_id=peer(n), device_id_type=MESH)

    def total_to(d):
        return pltpu.make_async_remote_copy(TL, TB.at[me], tsend.at[d], trecv.at[d], device_id=peer((me + d) % 32), device_id_type=MESH)

    turn = (x * (big + 1)) // 4

    def jstep(t, carry):
        jb = jnp.where(t + turn > big, t + turn - big - 1, t + turn)
        for h in range(64):
            vv = V[jb // 2, jb % 2, :, (h // 8) * 128:(h // 8 + 1) * 128]
            oo = jnp.concatenate([OC[a, h // 16, (h % 16) * 128:(h % 16 + 1) * 128, :] for a in (0, 1)], axis=1)
            im = jnp.dot(vv, oo, preferred_element_type=F32)
            for a in (0, 1):
                IM[a, pl.ds(h, 128, stride=IS), :] = im[:, a * 128:(a + 1) * 128]

        def contrib(t, slot):
            zero = jnp.zeros((64, 128), BF)
            PU = 64

            def pairs(n, carry):
                got = []
                for u in range(PU):
                    j = n * (2 * PU) + 2 * u
                    r0 = pl.multiple_of(n * (2 * PU * IS), 8)
                    lhs = jnp.concatenate([jnp.concatenate([IM[a, pl.ds(r0 + (2 * u + b) * IS, 64), :].astype(BF) for b in (0, 1)], axis=0) for a in (0, 1)], axis=1)
                    rhs = jnp.concatenate([
                        jnp.concatenate([W[t, j], zero], axis=1),
                        jnp.concatenate([zero, W[t, j + 1]], axis=1)], axis=0)
                    cc = lax.dot_general(lhs, rhs, (((0,), (0,)), ((), ())), preferred_element_type=F32)
                    r = jnp.sum(jnp.abs(cc), axis=0, keepdims=True)
                    got += [r[:, :128], r[:, 128:]]
                for b in range(PU // 4):
                    part[slot, pl.ds(pl.multiple_of(jb * 128 + n * (2 * PU) + 8 * b, 8), 8), :] = jnp.concatenate(got[8 * b:8 * b + 8], axis=0)
                return carry
            lax.fori_loop(0, 128 // (2 * PU), pairs, 0)
        contrib(jb, 1)

        @pl.when(jb <= p)
        def _():
            contrib(big + 1 + jb, 0)

        @pl.when(t == 0)
        def _():
            pl.semaphore_wait(ready, 3)

        @pl.when(t == 1)
        def _():
            for cp in remote:
                cp.wait_send()

            @pl.when(jnp.logical_not(stays))
            def _():
                for cp in move:
                    cp.wait_send()
        for w in range(4):
            n = jb * 4 + w

            @pl.when(n != me)
            def _():
                block_to(n).start()
        return carry
    lax.fori_loop(0, big + 1, jstep, 0)

    tl = jnp.concatenate([jnp.sum(part[a].reshape(128, 8, 128), axis=0) for a in (0, 1)], axis=0)
    TL[...] = tl
    TB[me] = tl

    def tell(d, carry):
        total_to(d).start()
        return carry
    lax.fori_loop(1, 32, tell, 0)
    RB[me] = part[:, pl.ds(pl.multiple_of(me * 32, 32), 32), :]

    def heard(d, carry):
        total_to(d).wait()
        return carry

    def sent(n, carry):
        @pl.when(n != me)
        def _():
            block_to(n).wait_send()
        return carry

    def scale(tb, a, ib):
        total = jnp.sum(tb[8 * a:8 * a + 8], axis=0, keepdims=True)
        pos = (ib * 128 + 1 + lax.broadcasted_iota(jnp.int32, (1, 128), 1)).astype(F32)
        return pos / total

    @pl.when(s <= big)
    def _():
        def take(n, carry):
            @pl.when(n != me)
            def _():
                block_from(n).wait_recv()
            return carry
        lax.fori_loop(0, 32, take, 0)
        NB[...] = jnp.sum(RB[...], axis=0)

    @pl.when(s > big)
    def _():
        NB[...] = jnp.zeros(NB.shape, F32)
    lax.fori_loop(1, 32, heard, 0)
    tb = jnp.sum(TB[...], axis=0)
    for a, ib in ((0, p), (1, big)):
        NB[a] = NB[a] * scale(tb, a, ib)

    def home(a):
        ib = (p, big)[a]
        return ib // 2, ib % 2, pltpu.make_async_remote_copy(NB.at[a], out.at[ib % 2], wsend.at[a], wrecv.at[ib % 2], device_id={**at, "row": ib // 2}, device_id_type=MESH)

    for a in (0, 1):
        owner, half, cp = home(a)

        @pl.when(owner == y)
        def _():
            out[half] = NB[a]

        @pl.when(owner != y)
        def _():
            cp.start()
    lax.fori_loop(0, (big + 1) * 4, sent, 0)
    for h in (0, 1):
        ib = y * 2 + h
        came = mixed(jnp.where(ib < 4, ib, 7 - ib), x)

        @pl.when(came != y)
        def _():
            pltpu.make_async_remote_copy(NB.at[h], out.at[h], wsend.at[h], wrecv.at[h], device_id={**at, "row": came}, device_id_type=MESH).wait_recv()
    for a in (0, 1):
        owner, half, cp = home(a)

        @pl.when(owner != y)
        def _():
            cp.wait_send()


def body(query_rows, key_rows, value_rows, out_proj):
    hbm = pl.BlockSpec(memory_space=pl.ANY)
    D = pltpu.SemaphoreType.DMA
    out = pl.pallas_call(
        layer_kernel, out_shape=jax.ShapeDtypeStruct((2, 32, 128), F32), in_specs=[hbm] * 4,
        out_specs=pl.BlockSpec(memory_space=pltpu.VMEM),
        scratch_shapes=[
            pltpu.VMEM((4, 2, 128, 2048), BF), pltpu.VMEM((4, 4, 2, 128, 256), BF), pltpu.VMEM((4, 2, 128, 1024), BF), pltpu.VMEM((2, 4, 2048, 128), BF),
            *SCR, pltpu.VMEM((2, 1024, 128), F32), pltpu.VMEM((32, 2, 32, 128), F32), pltpu.VMEM((32, 16, 128), F32),
            pltpu.VMEM((16, 128), F32), pltpu.VMEM((2, 32, 128), F32),
            D((80,)), D((80,)), D((8,)), D((32,)), D((32,)), D((32,)), D((32,)), D((2,)), D((2,)), pltpu.SemaphoreType.REGULAR],
        compiler_params=pltpu.CompilerParams(collective_id=0, has_side_effects=True, vmem_limit_bytes=62 * 2**20),
    )(query_rows, key_rows, value_rows, out_proj)
    return out.transpose(0, 2, 1).reshape(256, 32)


def solution(mesh):
    placed = (PS_("row", "width"), PS_("src", "width"), PS_("src", None), PS_(("row", "src"), "width"))
    return jax.shard_map(
        body, mesh=mesh, in_specs=placed, out_specs=PS_("row", ("src", "width")), check_vma=False
    )
```

```python
import math
import jax, jax.numpy as jnp
from jax import lax
from jax.experimental import pallas as pl
from jax.experimental.pallas import tpu as pltpu
from jax.sharding import PartitionSpec as PS_
C2 = math.log2(math.e) / math.sqrt(128.0)
F32, BF = jnp.float32, jnp.bfloat16
NEG = -1e30
PS, IS = 17, 65

SCR = [pltpu.VMEM((8, 128 * PS, 128), F32), pltpu.VMEM((9, 128, 64, 128), BF),
       pltpu.VMEM((8, 16, 128), F32), pltpu.VMEM((8, 16, 128), F32), pltpu.VMEM((8, 16, 128), F32),
       pltpu.VMEM((2, 128 * IS, 128), F32)]


MESH = pl.DeviceIdType.MESH


def mixed(a, b):
    return (a // 2 + b // 2) % 2 * 2 + (a + b) % 2


class Links:
    def __init__(self, send, recv, at=None):
        self.send, self.recv, self.n, self.at = send, recv, 0, at

    def to(self, source, target, **where):
        i = self.n
        self.n += 1
        return pltpu.make_async_remote_copy(src_ref=source, dst_ref=target, send_sem=self.send.at[i], recv_sem=self.recv.at[i],
                                            device_id={**self.at, **where}, device_id_type=MESH)


def layer_kernel(qi, ki, vi, oi, out, Q, K, V, OC, P, W, MS, LS, FS, IM, part, RB, TB, TL, NB,
                 send, recv, local, rsend, rrecv, tsend, trecv, wsend, wrecv, ready):
    z, y, s = lax.axis_index("width"), lax.axis_index("row"), lax.axis_index("src")
    x, c = s // 2, s % 2
    me = s * 4 + z
    p = mixed(x, y)
    big = 7 - p
    at = {"width": z, "row": y, "src": s}
    zu, zd, zf = (z + 1) % 4, (z + 3) % 4, (z + 2) % 4
    yu, yd = (y + 1) % 4, (y + 3) % 4
    xu, xd, xf = (x + 1) % 4, (x + 3) % 4, (x + 2) % 4
    su, sd, sib = xu * 2 + c, xd * 2 + c, x * 2 + 1 - c

    barrier = pltpu.get_barrier_semaphore()

    def peer(n):
        return {"width": n % 4, "row": mixed(p, n // 8), "src": n // 4}

    def greet(**where):
        pl.semaphore_signal(barrier, inc=1, device_id={**at, **where}, device_id_type=MESH)

    for d in range(1, 8):
        greet(src=(s + d) % 8)
    for d in range(1, 4):
        for b in (0, 1):
            greet(row=(y + d) % 4, src=x * 2 + b)
    for w in (zu, zd, zf):
        greet(width=w)

    links = Links(send, recv, at)
    to = links.to

    def both(ref, *wheres):
        return [to(ref, ref, **w) for w in wheres]

    rows = y * 2 + c
    pair = jnp.where(rows < 4, rows, 7 - rows)
    goal, slot_to = mixed(pair, x), y // 2
    stays = jnp.logical_and(goal == y, slot_to == c)
    q_half = qi.at[pl.ds(c * 128, 128), :]
    move = [to(q_half.at[pl.ds(h * 64, 64), :], Q.at[z, slot_to, pl.ds(h * 64, 64)], row=goal, src=x * 2 + slot_to) for h in (0, 1)]
    keep = pltpu.make_async_copy(q_half, Q.at[z, c], local.at[0])

    def o_src(b):
        return oi.at[:, pl.ds(b * 128, 128)]

    def o_dst(ch):
        return OC.at[ch, y, pl.ds(s * 256, 256), :]
    loc_k = pltpu.make_async_copy(ki, K.at[z, x, c], local.at[1])
    loc_v = pltpu.make_async_copy(vi, V.at[x, c], local.at[2])
    loc_o = [pltpu.make_async_copy(o_src(s), o_dst(0), local.at[3]), pltpu.make_async_copy(o_src(8 + y * 2 + c), o_dst(1), local.at[4])]
    kx = [to(ki, K.at[z, x, c], src=(s + d) % 8) for d in (2, 4, 6)]
    vx = [to(vi, V.at[x, c], src=w) for w in (su, sd, sib)]
    oa = [to(o_src((s + d) % 8), o_dst(0), src=(s + d) % 8) for d in range(1, 8)]
    ob = [to(o_src(8 + ((y + d) % 4) * 2 + (c + b) % 2), o_dst(1), row=(y + d) % 4, src=x * 2 + (c + b) % 2) for d in range(1, 4) for b in (0, 1)]
    ob += [to(o_src(8 + y * 2 + 1 - c), o_dst(1), src=sib)]
    ups, downs, other = dict(width=zu), dict(width=zd), dict(src=sib)
    kz = both(K.at[z, :, c], ups, downs)
    qz = [both(Q.at[z, c, pl.ds(h * 64, 64)], ups, downs) for h in (0, 1)]
    kf = both(K.at[zd, pl.ds(0, 2), c], ups) + both(K.at[zu, pl.ds(2, 2), c], downs)
    vf = both(V.at[xd, c, pl.ds(0, 64)], dict(src=su)) + both(V.at[xu, c, pl.ds(64, 64)], dict(src=sd))
    qf = both(Q.at[zd, c, pl.ds(0, 64)], ups) + both(Q.at[zu, c, pl.ds(64, 64)], downs)
    kg = [both(K.at[a, :, c], other)[0] for a in (z, zd, zu, zf)]
    vg = [both(V.at[a, c], other)[0] for a in (xd, xu, xf)]
    qs = [both(Q.at[a, c], other)[0] for a in (z, zd, zu, zf)]
    oy = both(OC.at[0, y], dict(row=yu), dict(row=yd))
    oyf = both(OC.at[0, yd, pl.ds(0, 1024)], dict(row=yu)) + both(OC.at[0, yu, pl.ds(1024, 1024)], dict(row=yd))
    ow = both(OC.at[1, :, pl.ds(x * 512, 512)], dict(src=su), dict(src=sd))
    owf = both(OC.at[1, pl.ds(0, 2), pl.ds(xd * 512, 512)], dict(src=su)) + both(OC.at[1, pl.ds(2, 2), pl.ds(xu * 512, 512)], dict(src=sd))
    remote = kx + vx + oa + ob + kz + qz[0] + qz[1] + kf + vf + qf + kg + vg + qs + oy + oyf + ow + owf

    def start(*copies):
        for cp in copies:
            cp.start()

    def arrived(*copies):
        for cp in copies:
            cp.wait_recv()

    start(loc_k, *loc_o, loc_v)
    part[...] = jnp.zeros(part.shape, F32)
    pl.semaphore_wait(barrier, 16)
    start(*kx)

    @pl.when(stays)
    def _():
        keep.start()

    @pl.when(jnp.logical_not(stays))
    def _():
        start(*move)
    start(*oa)
    loc_k.wait()
    arrived(*kx)
    start(*kz, kg[0])
    start(*ob, *vx)

    @pl.when(stays)
    def _():
        keep.wait()

    for h in (0, 1):
        @pl.when(jnp.logical_not(stays))
        def _():
            arrived(move[h])
        start(*qz[h])
    start(qs[0])
    for cp in loc_o:
        cp.wait()
    loc_v.wait()
    arrived(*oa)
    start(*oy)
    arrived(*ob)
    start(*ow)
    for h in (0, 1):
        arrived(kz[h])
        start(kf[h], kg[1 + h])
    for h in (0, 1):
        arrived(vx[h])
        start(vf[h], vg[h])
    arrived(qz[0][0])
    start(qf[0])
    arrived(kg[0], qs[0])

    jl = lax.broadcasted_iota(jnp.int32, (128, 256), 0)
    il = lax.broadcasted_iota(jnp.int32, (128, 256), 1) % 128

    def scores(zc, slot, ib, base):
        MS[...] = jnp.full(MS.shape, NEG, F32)
        LS[...] = jnp.zeros(LS.shape, F32)

        def block(jb, diag):
            for hp in range(8):
                kk = K[zc, jb // 2, jb % 2, :, (hp // 4) * 128:(hp // 4 + 1) * 128]
                qq = jnp.concatenate([Q[zc, slot, :, (2 * hp + a) * 128:(2 * hp + a + 1) * 128] for a in (0, 1)], axis=0)
                sc = lax.dot_general(kk, qq, (((1,), (1,)), ((), ())), preferred_element_type=F32)
                if diag:
                    sc = jnp.where(jl <= il, sc, NEG)
                m = jnp.max(sc, axis=0, keepdims=True)
                e = jnp.exp2((sc - m) * C2)
                l = jnp.sum(e, axis=0, keepdims=True)
                for a in (0, 1):
                    lanes = slice(a * 128, (a + 1) * 128)
                    P[jb, pl.ds(2 * hp + a, 128, stride=PS), :] = e[:, lanes]
                    MS[jb, 2 * hp + a:2 * hp + a + 1, :] = m[:, lanes]
                    LS[jb, 2 * hp + a:2 * hp + a + 1, :] = l[:, lanes]

        def plain(jb, carry):
            block(jb, False)
            return carry
        lax.fori_loop(0, ib, plain, 0)
        block(ib, True)
        ms = MS[...]
        f = jnp.exp2((ms - jnp.max(ms, axis=0, keepdims=True)) * C2)
        total = jnp.sum(f * LS[...], axis=0, keepdims=True)
        FS[...] = f / total

        def conv(jb, carry):
            fs = FS[jb]
            for j in range(128):
                W[base + jb, j, pl.ds(pl.multiple_of(zc * 16, 16), 16), :] = (P[jb, j * PS:j * PS + 16, :] * fs).astype(BF)
            return carry
        lax.fori_loop(0, ib + 1, conv, 0)

    def zstep(d, carry):
        @pl.when(d == 1)
        def _():
            arrived(qz[0][1], qz[1][1])
            start(qf[1], qs[2])
            arrived(qz[1][0])
            start(qs[1])
            for h in (0, 1):
                arrived(oy[h])
                start(oyf[h])
            for h in (0, 1):
                arrived(ow[h])
                start(owf[h])
            arrived(kg[1], qs[1])

        @pl.when(d == 2)
        def _():
            arrived(*kf)
            start(kg[3])
            arrived(*vf)
            start(vg[2])
            arrived(kg[2], qs[2])

        @pl.when(d == 3)
        def _():
            arrived(*qf)
            start(qs[3])
            arrived(kg[3], qs[3])
        zc = (z + jnp.where(d == 1, 3, jnp.where(d == 2, 1, jnp.where(d == 3, 2, 0)))) % 4
        scores(zc, 0, p, big + 1)
        scores(zc, 1, big, 0)
        return carry
    lax.fori_loop(0, 4, zstep, 0)

    arrived(vx[2], *vg, *oyf, *owf)
    for w in (zu, zd, zf):
        pl.semaphore_signal(ready, inc=1, device_id={**at, "width": w}, device_id_type=MESH)

    def block_to(n):
        return pltpu.make_async_remote_copy(part.at[:, pl.ds(n * 32, 32), :], RB.at[me], rsend.at[n], rrecv, device_id=peer(n), device_id_type=MESH)

    def first_to(d):
        return pltpu.make_async_remote_copy(TL.at[0], TB.at[z], tsend.at[d], trecv.at[d], device_id={**at, "width": (z + d) % 4}, device_id_type=MESH)

    def second_to(d):
        n = (s + d) % 8
        return pltpu.make_async_remote_copy(TL.at[1], TB.at[4 + s], tsend.at[4 + d], trecv.at[4 + d], device_id={"width": z, "row": mixed(p, n // 2), "src": n}, device_id_type=MESH)

    turn = (x * (big + 1)) // 4

    def jstep(t, carry):
        jb = jnp.where(t + turn > big, t + turn - big - 1, t + turn)
        for h in range(64):
            vv = V[jb // 2, jb % 2, :, (h // 8) * 128:(h // 8 + 1) * 128]
            oo = jnp.concatenate([OC[a, h // 16, (h % 16) * 128:(h % 16 + 1) * 128, :] for a in (0, 1)], axis=1)
            im = jnp.dot(vv, oo, preferred_element_type=F32)
            for a in (0, 1):
                IM[a, pl.ds(h, 128, stride=IS), :] = im[:, a * 128:(a + 1) * 128]

        def contrib(t, slot):
            zero = jnp.zeros((64, 128), BF)
            PU = 64

            def pairs(n, carry):
                got = []
                for u in range(PU):
                    j = n * (2 * PU) + 2 * u
                    r0 = pl.multiple_of(n * (2 * PU * IS), 8)
                    lhs = jnp.concatenate([jnp.concatenate([IM[a, pl.ds(r0 + (2 * u + b) * IS, 64), :].astype(BF) for b in (0, 1)], axis=0) for a in (0, 1)], axis=1)
                    rhs = jnp.concatenate([
                        jnp.concatenate([W[t, j], zero], axis=1),
                        jnp.concatenate([zero, W[t, j + 1]], axis=1)], axis=0)
                    cc = lax.dot_general(lhs, rhs, (((0,), (0,)), ((), ())), preferred_element_type=F32)
                    r = jnp.sum(jnp.abs(cc), axis=0, keepdims=True)
                    got += [r[:, :128], r[:, 128:]]
                for b in range(PU // 4):
                    part[slot, pl.ds(pl.multiple_of(jb * 128 + n * (2 * PU) + 8 * b, 8), 8), :] = jnp.concatenate(got[8 * b:8 * b + 8], axis=0)
                return carry
            lax.fori_loop(0, 128 // (2 * PU), pairs, 0)
        contrib(jb, 1)

        @pl.when(jb <= p)
        def _():
            contrib(big + 1 + jb, 0)

        @pl.when(t == 0)
        def _():
            pl.semaphore_wait(ready, 3)

        @pl.when(t == 1)
        def _():
            for cp in remote:
                cp.wait_send()

            @pl.when(jnp.logical_not(stays))
            def _():
                for cp in move:
                    cp.wait_send()
        for w in range(4):
            n = jb * 4 + w

            @pl.when(n != me)
            def _():
                block_to(n).start()
        return carry
    lax.fori_loop(0, big + 1, jstep, 0)

    tl = jnp.concatenate([jnp.sum(part[a].reshape(128, 8, 128), axis=0) for a in (0, 1)], axis=0)
    TL[0] = tl
    firsts = [first_to(d) for d in range(1, 4)]
    seconds = [second_to(d) for d in range(1, 8)]
    start(*firsts)
    TB[z] = tl

    @pl.when(s <= big)
    def _():
        RB[me] = part[:, pl.ds(pl.multiple_of(me * 32, 32), 32), :]
    arrived(*firsts)
    tl = jnp.sum(TB[0:4], axis=0)
    TL[1] = tl
    start(*seconds)
    TB[4 + s] = tl

    def sent(n, carry):
        @pl.when(n != me)
        def _():
            block_to(n).wait_send()
        return carry

    def scale(tb, a, ib):
        total = jnp.sum(tb[8 * a:8 * a + 8], axis=0, keepdims=True)
        pos = (ib * 128 + 1 + lax.broadcasted_iota(jnp.int32, (1, 128), 1)).astype(F32)
        return pos / total

    @pl.when(s <= big)
    def _():
        pltpu.make_async_remote_copy(RB.at[pl.ds(0, 31)], RB.at[pl.ds(0, 31)], rsend.at[0], rrecv, device_id=at, device_id_type=MESH).wait_recv()
        NB[...] = jnp.sum(RB[...], axis=0)

    @pl.when(s > big)
    def _():
        NB[...] = jnp.zeros(NB.shape, F32)
    arrived(*seconds)
    tb = jnp.sum(TB[4:12], axis=0)
    for a, ib in ((0, p), (1, big)):
        NB[a] = NB[a] * scale(tb, a, ib)

    def home(a):
        ib = (p, big)[a]
        return ib // 2, ib % 2, pltpu.make_async_remote_copy(NB.at[a], out.at[ib % 2], wsend.at[a], wrecv.at[ib % 2], device_id={**at, "row": ib // 2}, device_id_type=MESH)

    for a in (0, 1):
        owner, half, cp = home(a)

        @pl.when(owner == y)
        def _():
            out[half] = NB[a]

        @pl.when(owner != y)
        def _():
            cp.start()
    lax.fori_loop(0, (big + 1) * 4, sent, 0)
    for cp in firsts + seconds:
        cp.wait_send()
    for h in (0, 1):
        ib = y * 2 + h
        came = mixed(jnp.where(ib < 4, ib, 7 - ib), x)

        @pl.when(came != y)
        def _():
            pltpu.make_async_remote_copy(NB.at[h], out.at[h], wsend.at[h], wrecv.at[h], device_id={**at, "row": came}, device_id_type=MESH).wait_recv()
    for a in (0, 1):
        owner, half, cp = home(a)

        @pl.when(owner != y)
        def _():
            cp.wait_send()


def body(query_rows, key_rows, value_rows, out_proj):
    hbm = pl.BlockSpec(memory_space=pl.ANY)
    D = pltpu.SemaphoreType.DMA
    out = pl.pallas_call(
        layer_kernel, out_shape=jax.ShapeDtypeStruct((2, 32, 128), F32), in_specs=[hbm] * 4,
        out_specs=pl.BlockSpec(memory_space=pltpu.VMEM),
        scratch_shapes=[
            pltpu.VMEM((4, 2, 128, 2048), BF), pltpu.VMEM((4, 4, 2, 128, 256), BF), pltpu.VMEM((4, 2, 128, 1024), BF), pltpu.VMEM((2, 4, 2048, 128), BF),
            *SCR, pltpu.VMEM((2, 1024, 128), F32), pltpu.VMEM((32, 2, 32, 128), F32), pltpu.VMEM((12, 16, 128), F32),
            pltpu.VMEM((2, 16, 128), F32), pltpu.VMEM((2, 32, 128), F32),
            D((80,)), D((80,)), D((8,)), D((32,)), D, D((12,)), D((12,)), D((2,)), D((2,)), pltpu.SemaphoreType.REGULAR],
        compiler_params=pltpu.CompilerParams(collective_id=0, has_side_effects=True, vmem_limit_bytes=62 * 2**20),
    )(query_rows, key_rows, value_rows, out_proj)
    return out.transpose(0, 2, 1).reshape(256, 32)


def solution(mesh):
    placed = (PS_("row", "width"), PS_("src", "width"), PS_("src", None), PS_(("row", "src"), "width"))
    return jax.shard_map(
        body, mesh=mesh, in_specs=placed, out_specs=PS_("row", ("src", "width")), check_vma=False
    )
```

```python
import math
import jax, jax.numpy as jnp
from jax import lax
from jax.experimental import pallas as pl
from jax.experimental.pallas import tpu as pltpu
from jax.sharding import PartitionSpec as PS_
C2 = math.log2(math.e) / math.sqrt(128.0)
F32, BF = jnp.float32, jnp.bfloat16
NEG = -1e30
PS, IS = 17, 65

SCR = [pltpu.VMEM((8, 128 * PS, 128), F32), pltpu.VMEM((9, 128, 64, 128), BF),
       pltpu.VMEM((8, 16, 128), F32), pltpu.VMEM((8, 16, 128), F32), pltpu.VMEM((8, 16, 128), F32),
       pltpu.VMEM((2, 128 * IS, 128), F32)]


MESH = pl.DeviceIdType.MESH


def mixed(a, b):
    return (a // 2 + b // 2) % 2 * 2 + (a + b) % 2


class Links:
    def __init__(self, send, recv, at=None):
        self.send, self.recv, self.n, self.at = send, recv, 0, at

    def to(self, source, target, **where):
        i = self.n
        self.n += 1
        return pltpu.make_async_remote_copy(src_ref=source, dst_ref=target, send_sem=self.send.at[i], recv_sem=self.recv.at[i],
                                            device_id={**self.at, **where}, device_id_type=MESH)


def layer_kernel(qi, ki, vi, oi, out, Q, K, V, OC, P, W, MS, LS, FS, IM, part, RB, TB, TL, NB,
                 send, recv, local, rsend, rrecv, tsend, trecv, wsend, wrecv, ready):
    z, y, s = lax.axis_index("width"), lax.axis_index("row"), lax.axis_index("src")
    x, c = s // 2, s % 2
    me = s * 4 + z
    p = mixed(x, y)
    big = 7 - p
    at = {"width": z, "row": y, "src": s}
    zu, zd, zf = (z + 1) % 4, (z + 3) % 4, (z + 2) % 4
    yu, yd = (y + 1) % 4, (y + 3) % 4
    xu, xd, xf = (x + 1) % 4, (x + 3) % 4, (x + 2) % 4
    su, sd, sib = xu * 2 + c, xd * 2 + c, x * 2 + 1 - c

    barrier = pltpu.get_barrier_semaphore()

    def peer(n):
        return {"width": n % 4, "row": mixed(p, n // 8), "src": n // 4}

    def greet(**where):
        pl.semaphore_signal(barrier, inc=1, device_id={**at, **where}, device_id_type=MESH)

    for d in range(1, 8):
        greet(src=(s + d) % 8)
    for d in range(1, 4):
        for b in (0, 1):
            greet(row=(y + d) % 4, src=x * 2 + b)
    for w in (zu, zd, zf):
        greet(width=w)

    links = Links(send, recv, at)
    to = links.to

    def both(ref, *wheres):
        return [to(ref, ref, **w) for w in wheres]

    rows = y * 2 + c
    pair = jnp.where(rows < 4, rows, 7 - rows)
    goal, slot_to = mixed(pair, x), y // 2
    stays = jnp.logical_and(goal == y, slot_to == c)
    q_half = qi.at[pl.ds(c * 128, 128), :]
    move = [to(q_half.at[pl.ds(h * 64, 64), :], Q.at[z, slot_to, pl.ds(h * 64, 64)], row=goal, src=x * 2 + slot_to) for h in (0, 1)]
    keep = pltpu.make_async_copy(q_half, Q.at[z, c], local.at[0])

    def o_src(b):
        return oi.at[:, pl.ds(b * 128, 128)]

    def o_dst(ch):
        return OC.at[ch, y, pl.ds(s * 256, 256), :]
    loc_k = pltpu.make_async_copy(ki, K.at[z, x, c], local.at[1])
    loc_v = pltpu.make_async_copy(vi, V.at[x, c], local.at[2])
    loc_o = [pltpu.make_async_copy(o_src(s), o_dst(0), local.at[3]), pltpu.make_async_copy(o_src(8 + y * 2 + c), o_dst(1), local.at[4])]
    kx = [to(ki, K.at[z, x, c], src=(s + d) % 8) for d in (2, 4, 6)]
    vx = [to(vi, V.at[x, c], src=w) for w in (su, sd, sib)]
    oa = [to(o_src((s + d) % 8), o_dst(0), src=(s + d) % 8) for d in range(1, 8)]
    ob = [to(o_src(8 + ((y + d) % 4) * 2 + (c + b) % 2), o_dst(1), row=(y + d) % 4, src=x * 2 + (c + b) % 2) for d in range(1, 4) for b in (0, 1)]
    ob += [to(o_src(8 + y * 2 + 1 - c), o_dst(1), src=sib)]
    ups, downs, other = dict(width=zu), dict(width=zd), dict(src=sib)
    kz = both(K.at[z, :, c], ups, downs)
    qz = [both(Q.at[z, c, pl.ds(h * 64, 64)], ups, downs) for h in (0, 1)]
    kf = both(K.at[zd, pl.ds(0, 2), c], ups) + both(K.at[zu, pl.ds(2, 2), c], downs)
    vf = both(V.at[xd, c, pl.ds(0, 64)], dict(src=su)) + both(V.at[xu, c, pl.ds(64, 64)], dict(src=sd))
    qf = both(Q.at[zd, c, pl.ds(0, 64)], ups) + both(Q.at[zu, c, pl.ds(64, 64)], downs)
    kg = [both(K.at[a, :, c], other)[0] for a in (z, zd, zu, zf)]
    vg = [both(V.at[a, c], other)[0] for a in (xd, xu, xf)]
    qs = [both(Q.at[a, c], other)[0] for a in (z, zd, zu, zf)]
    oy = both(OC.at[0, y], dict(row=yu), dict(row=yd))
    oyf = both(OC.at[0, yd, pl.ds(0, 1024)], dict(row=yu)) + both(OC.at[0, yu, pl.ds(1024, 1024)], dict(row=yd))
    ow = both(OC.at[1, :, pl.ds(x * 512, 512)], dict(src=su), dict(src=sd))
    owf = both(OC.at[1, pl.ds(0, 2), pl.ds(xd * 512, 512)], dict(src=su)) + both(OC.at[1, pl.ds(2, 2), pl.ds(xu * 512, 512)], dict(src=sd))
    remote = kx + vx + oa + ob + kz + qz[0] + qz[1] + kf + vf + qf + kg + vg + qs + oy + oyf + ow + owf

    def start(*copies):
        for cp in copies:
            cp.start()

    def arrived(*copies):
        for cp in copies:
            cp.wait_recv()

    start(loc_k, *loc_o, loc_v)
    part[...] = jnp.zeros(part.shape, F32)
    pl.semaphore_wait(barrier, 16)
    start(*kx)

    @pl.when(stays)
    def _():
        keep.start()

    @pl.when(jnp.logical_not(stays))
    def _():
        start(*move)
    start(*oa)
    loc_k.wait()
    arrived(*kx)
    start(*kz, kg[0])
    start(*ob, *vx)

    @pl.when(stays)
    def _():
        keep.wait()

    for h in (0, 1):
        @pl.when(jnp.logical_not(stays))
        def _():
            arrived(move[h])
        start(*qz[h])
    start(qs[0])
    for cp in loc_o:
        cp.wait()
    loc_v.wait()
    arrived(*oa)
    start(*oy)
    arrived(*ob)
    start(*ow)
    for h in (0, 1):
        arrived(kz[h])
        start(kf[h], kg[1 + h])
    for h in (0, 1):
        arrived(vx[h])
        start(vf[h], vg[h])
    arrived(qz[0][0])
    start(qf[0])
    arrived(kg[0], qs[0])

    jl = lax.broadcasted_iota(jnp.int32, (128, 256), 0)
    il = lax.broadcasted_iota(jnp.int32, (128, 256), 1) % 128

    def scores(zc, slot, ib, base):
        MS[...] = jnp.full(MS.shape, NEG, F32)
        LS[...] = jnp.zeros(LS.shape, F32)

        def block(jb, diag):
            for hp in range(8):
                kk = K[zc, jb // 2, jb % 2, :, (hp // 4) * 128:(hp // 4 + 1) * 128]
                qq = jnp.concatenate([Q[zc, slot, :, (2 * hp + a) * 128:(2 * hp + a + 1) * 128] for a in (0, 1)], axis=0)
                sc = lax.dot_general(kk, qq, (((1,), (1,)), ((), ())), preferred_element_type=F32)
                if diag:
                    sc = jnp.where(jl <= il, sc, NEG)
                m = jnp.max(sc, axis=0, keepdims=True)
                e = jnp.exp2((sc - m) * C2)
                l = jnp.sum(e, axis=0, keepdims=True)
                for a in (0, 1):
                    lanes = slice(a * 128, (a + 1) * 128)
                    P[jb, pl.ds(2 * hp + a, 128, stride=PS), :] = e[:, lanes]
                    MS[jb, 2 * hp + a:2 * hp + a + 1, :] = m[:, lanes]
                    LS[jb, 2 * hp + a:2 * hp + a + 1, :] = l[:, lanes]

        def plain(jb, carry):
            block(jb, False)
            return carry
        lax.fori_loop(0, ib, plain, 0)
        block(ib, True)
        ms = MS[...]
        f = jnp.exp2((ms - jnp.max(ms, axis=0, keepdims=True)) * C2)
        total = jnp.sum(f * LS[...], axis=0, keepdims=True)
        FS[...] = f / total

        def conv(jb, carry):
            fs = FS[jb]
            for j in range(128):
                W[base + jb, j, pl.ds(pl.multiple_of(zc * 16, 16), 16), :] = (P[jb, j * PS:j * PS + 16, :] * fs).astype(BF)
            return carry
        lax.fori_loop(0, ib + 1, conv, 0)

    turn = (x * (big + 1)) // 4

    def source(t):
        return jnp.where(t + turn > big, t + turn - big - 1, t + turn)

    def images(t):
        jb = source(t)
        for h in range(64):
            vv = V[jb // 2, jb % 2, :, (h // 8) * 128:(h // 8 + 1) * 128]
            oo = jnp.concatenate([OC[a, h // 16, (h % 16) * 128:(h % 16 + 1) * 128, :] for a in (0, 1)], axis=1)
            im = jnp.dot(vv, oo, preferred_element_type=F32)
            for a in (0, 1):
                IM[a, pl.ds(h, 128, stride=IS), :] = im[:, a * 128:(a + 1) * 128]

    def zstep(d, carry):
        @pl.when(d == 1)
        def _():
            arrived(qz[0][1], qz[1][1])
            start(qf[1], qs[2])
            arrived(qz[1][0])
            start(qs[1])
            for h in (0, 1):
                arrived(oy[h])
                start(oyf[h])
            for h in (0, 1):
                arrived(ow[h])
                start(owf[h])
            arrived(kg[1], qs[1])

        @pl.when(d == 2)
        def _():
            arrived(*kf)
            start(kg[3])
            arrived(*vf)
            start(vg[2])
            arrived(kg[2], qs[2])

        @pl.when(d == 3)
        def _():
            arrived(*qf)
            start(qs[3])
            arrived(kg[3], vx[2], *vg, *oyf, *owf)
            images(0)
            arrived(qs[3])
        zc = (z + jnp.where(d == 1, 3, jnp.where(d == 2, 1, jnp.where(d == 3, 2, 0)))) % 4
        scores(zc, 0, p, big + 1)
        scores(zc, 1, big, 0)
        return carry
    lax.fori_loop(0, 4, zstep, 0)

    for w in (zu, zd, zf):
        pl.semaphore_signal(ready, inc=1, device_id={**at, "width": w}, device_id_type=MESH)

    def block_to(n):
        return pltpu.make_async_remote_copy(part.at[:, pl.ds(n * 32, 32), :], RB.at[me], rsend.at[n], rrecv, device_id=peer(n), device_id_type=MESH)

    def first_to(d):
        return pltpu.make_async_remote_copy(TL.at[0], TB.at[z], tsend.at[d], trecv.at[d], device_id={**at, "width": (z + d) % 4}, device_id_type=MESH)

    def second_to(d):
        n = (s + d) % 8
        return pltpu.make_async_remote_copy(TL.at[1], TB.at[4 + s], tsend.at[4 + d], trecv.at[4 + d], device_id={"width": z, "row": mixed(p, n // 2), "src": n}, device_id_type=MESH)


    def jstep(t, carry):
        jb = source(t)

        def contrib(t, slot):
            zero = jnp.zeros((64, 128), BF)
            PU = 64

            def pairs(n, carry):
                got = []
                for u in range(PU):
                    j = n * (2 * PU) + 2 * u
                    r0 = pl.multiple_of(n * (2 * PU * IS), 8)
                    lhs = jnp.concatenate([jnp.concatenate([IM[a, pl.ds(r0 + (2 * u + b) * IS, 64), :].astype(BF) for b in (0, 1)], axis=0) for a in (0, 1)], axis=1)
                    rhs = jnp.concatenate([
                        jnp.concatenate([W[t, j], zero], axis=1),
                        jnp.concatenate([zero, W[t, j + 1]], axis=1)], axis=0)
                    cc = lax.dot_general(lhs, rhs, (((0,), (0,)), ((), ())), preferred_element_type=F32)
                    r = jnp.sum(jnp.abs(cc), axis=0, keepdims=True)
                    got += [r[:, :128], r[:, 128:]]
                for b in range(PU // 4):
                    part[slot, pl.ds(pl.multiple_of(jb * 128 + n * (2 * PU) + 8 * b, 8), 8), :] = jnp.concatenate(got[8 * b:8 * b + 8], axis=0)
                return carry
            lax.fori_loop(0, 128 // (2 * PU), pairs, 0)
        contrib(jb, 1)

        @pl.when(jb <= p)
        def _():
            contrib(big + 1 + jb, 0)

        @pl.when(t == 0)
        def _():
            pl.semaphore_wait(ready, 3)

        @pl.when(t == 1)
        def _():
            for cp in remote:
                cp.wait_send()

            @pl.when(jnp.logical_not(stays))
            def _():
                for cp in move:
                    cp.wait_send()
        for w in range(4):
            n = jb * 4 + w

            @pl.when(n != me)
            def _():
                block_to(n).start()

        @pl.when(t < big)
        def _():
            images(t + 1)
        return carry
    lax.fori_loop(0, big + 1, jstep, 0)

    tl = jnp.concatenate([jnp.sum(part[a].reshape(128, 8, 128), axis=0) for a in (0, 1)], axis=0)
    TL[0] = tl
    firsts = [first_to(d) for d in range(1, 4)]
    seconds = [second_to(d) for d in range(1, 8)]
    start(*firsts)
    TB[z] = tl

    @pl.when(s <= big)
    def _():
        RB[me] = part[:, pl.ds(pl.multiple_of(me * 32, 32), 32), :]
    arrived(*firsts)
    tl = jnp.sum(TB[0:4], axis=0)
    TL[1] = tl
    start(*seconds)
    TB[4 + s] = tl

    def sent(n, carry):
        @pl.when(n != me)
        def _():
            block_to(n).wait_send()
        return carry

    def scale(tb, a, ib):
        total = jnp.sum(tb[8 * a:8 * a + 8], axis=0, keepdims=True)
        pos = (ib * 128 + 1 + lax.broadcasted_iota(jnp.int32, (1, 128), 1)).astype(F32)
        return pos / total

    @pl.when(s <= big)
    def _():
        pltpu.make_async_remote_copy(RB.at[pl.ds(0, 31)], RB.at[pl.ds(0, 31)], rsend.at[0], rrecv, device_id=at, device_id_type=MESH).wait_recv()
        NB[...] = jnp.sum(RB[...], axis=0)

    @pl.when(s > big)
    def _():
        NB[...] = jnp.zeros(NB.shape, F32)
    arrived(*seconds)
    tb = jnp.sum(TB[4:12], axis=0)
    for a, ib in ((0, p), (1, big)):
        NB[a] = NB[a] * scale(tb, a, ib)

    def home(a):
        ib = (p, big)[a]
        return ib // 2, ib % 2, pltpu.make_async_remote_copy(NB.at[a], out.at[ib % 2], wsend.at[a], wrecv.at[ib % 2], device_id={**at, "row": ib // 2}, device_id_type=MESH)

    for a in (0, 1):
        owner, half, cp = home(a)

        @pl.when(owner == y)
        def _():
            out[half] = NB[a]

        @pl.when(owner != y)
        def _():
            cp.start()
    lax.fori_loop(0, (big + 1) * 4, sent, 0)
    for cp in firsts + seconds:
        cp.wait_send()
    for h in (0, 1):
        ib = y * 2 + h
        came = mixed(jnp.where(ib < 4, ib, 7 - ib), x)

        @pl.when(came != y)
        def _():
            pltpu.make_async_remote_copy(NB.at[h], out.at[h], wsend.at[h], wrecv.at[h], device_id={**at, "row": came}, device_id_type=MESH).wait_recv()
    for a in (0, 1):
        owner, half, cp = home(a)

        @pl.when(owner != y)
        def _():
            cp.wait_send()


def body(query_rows, key_rows, value_rows, out_proj):
    hbm = pl.BlockSpec(memory_space=pl.ANY)
    D = pltpu.SemaphoreType.DMA
    out = pl.pallas_call(
        layer_kernel, out_shape=jax.ShapeDtypeStruct((2, 32, 128), F32), in_specs=[hbm] * 4,
        out_specs=pl.BlockSpec(memory_space=pltpu.VMEM),
        scratch_shapes=[
            pltpu.VMEM((4, 2, 128, 2048), BF), pltpu.VMEM((4, 4, 2, 128, 256), BF), pltpu.VMEM((4, 2, 128, 1024), BF), pltpu.VMEM((2, 4, 2048, 128), BF),
            *SCR, pltpu.VMEM((2, 1024, 128), F32), pltpu.VMEM((32, 2, 32, 128), F32), pltpu.VMEM((12, 16, 128), F32),
            pltpu.VMEM((2, 16, 128), F32), pltpu.VMEM((2, 32, 128), F32),
            D((80,)), D((80,)), D((8,)), D((32,)), D, D((12,)), D((12,)), D((2,)), D((2,)), pltpu.SemaphoreType.REGULAR],
        compiler_params=pltpu.CompilerParams(collective_id=0, has_side_effects=True, vmem_limit_bytes=62 * 2**20),
    )(query_rows, key_rows, value_rows, out_proj)
    return out.transpose(0, 2, 1).reshape(256, 32)


def solution(mesh):
    placed = (PS_("row", "width"), PS_("src", "width"), PS_("src", None), PS_(("row", "src"), "width"))
    return jax.shard_map(
        body, mesh=mesh, in_specs=placed, out_specs=PS_("row", ("src", "width")), check_vma=False
    )
```

```python
import math
import jax, jax.numpy as jnp
from jax import lax
from jax.experimental import pallas as pl
from jax.experimental.pallas import tpu as pltpu
from jax.sharding import PartitionSpec as PS_
C2 = math.log2(math.e) / math.sqrt(128.0)
F32, BF = jnp.float32, jnp.bfloat16
NEG = -1e30
PS, IS = 17, 65

SCR = [pltpu.VMEM((8, 128 * PS + 16, 128), F32), pltpu.VMEM((9, 128, 64, 128), BF),
       pltpu.VMEM((8, 16, 128), F32), pltpu.VMEM((8, 16, 128), F32), pltpu.VMEM((8, 16, 128), F32),
       pltpu.VMEM((2, 128 * IS + 64, 128), F32)]


MESH = pl.DeviceIdType.MESH


def mixed(a, b):
    return (a // 2 + b // 2) % 2 * 2 + (a + b) % 2


class Links:
    def __init__(self, send, recv, at=None):
        self.send, self.recv, self.n, self.at = send, recv, 0, at

    def to(self, source, target, **where):
        i = self.n
        self.n += 1
        return pltpu.make_async_remote_copy(src_ref=source, dst_ref=target, send_sem=self.send.at[i], recv_sem=self.recv.at[i],
                                            device_id={**self.at, **where}, device_id_type=MESH)


def layer_kernel(qi, ki, vi, oi, out, Q, K, V, OC, P, W, MS, LS, FS, IM, part, RB, TB, TL, NB,
                 send, recv, local, rsend, rrecv, tsend, trecv, wsend, wrecv, ready):
    z, y, s = lax.axis_index("width"), lax.axis_index("row"), lax.axis_index("src")
    x, c = s // 2, s % 2
    me = s * 4 + z
    p = mixed(x, y)
    big = 7 - p
    at = {"width": z, "row": y, "src": s}
    zu, zd, zf = (z + 1) % 4, (z + 3) % 4, (z + 2) % 4
    yu, yd = (y + 1) % 4, (y + 3) % 4
    xu, xd, xf = (x + 1) % 4, (x + 3) % 4, (x + 2) % 4
    su, sd, sib = xu * 2 + c, xd * 2 + c, x * 2 + 1 - c

    barrier = pltpu.get_barrier_semaphore()

    def peer(n):
        return {"width": n % 4, "row": mixed(p, n // 8), "src": n // 4}

    def greet(**where):
        pl.semaphore_signal(barrier, inc=1, device_id={**at, **where}, device_id_type=MESH)

    for d in range(1, 8):
        greet(src=(s + d) % 8)
    for d in range(1, 4):
        for b in (0, 1):
            greet(row=(y + d) % 4, src=x * 2 + b)
    for w in (zu, zd, zf):
        greet(width=w)

    links = Links(send, recv, at)
    to = links.to

    def both(ref, *wheres):
        return [to(ref, ref, **w) for w in wheres]

    rows = y * 2 + c
    pair = jnp.where(rows < 4, rows, 7 - rows)
    goal, slot_to = mixed(pair, x), y // 2
    stays = jnp.logical_and(goal == y, slot_to == c)
    q_half = qi.at[pl.ds(c * 128, 128), :]
    move = [to(q_half.at[pl.ds(h * 64, 64), :], Q.at[z, slot_to, pl.ds(h * 64, 64)], row=goal, src=x * 2 + slot_to) for h in (0, 1)]
    keep = pltpu.make_async_copy(q_half, Q.at[z, c], local.at[0])

    def o_src(b):
        return oi.at[:, pl.ds(b * 128, 128)]

    def o_dst(ch):
        return OC.at[ch, y, pl.ds(s * 256, 256), :]
    loc_k = pltpu.make_async_copy(ki, K.at[z, x, c], local.at[1])
    loc_v = pltpu.make_async_copy(vi, V.at[x, c], local.at[2])
    loc_o = [pltpu.make_async_copy(o_src(s), o_dst(0), local.at[3]), pltpu.make_async_copy(o_src(8 + y * 2 + c), o_dst(1), local.at[4])]
    kx = [to(ki, K.at[z, x, c], src=(s + d) % 8) for d in (2, 4, 6)]
    vx = [to(vi, V.at[x, c], src=w) for w in (su, sd, sib)]
    oa = [to(o_src((s + d) % 8), o_dst(0), src=(s + d) % 8) for d in range(1, 8)]
    ob = [to(o_src(8 + ((y + d) % 4) * 2 + (c + b) % 2), o_dst(1), row=(y + d) % 4, src=x * 2 + (c + b) % 2) for d in range(1, 4) for b in (0, 1)]
    ob += [to(o_src(8 + y * 2 + 1 - c), o_dst(1), src=sib)]
    ups, downs, other = dict(width=zu), dict(width=zd), dict(src=sib)
    kz = both(K.at[z, :, c], ups, downs)
    qz = [both(Q.at[z, c, pl.ds(h * 64, 64)], ups, downs) for h in (0, 1)]
    kf = both(K.at[zd, pl.ds(0, 2), c], ups) + both(K.at[zu, pl.ds(2, 2), c], downs)
    vf = both(V.at[xd, c, pl.ds(0, 64)], dict(src=su)) + both(V.at[xu, c, pl.ds(64, 64)], dict(src=sd))
    qf = both(Q.at[zd, c, pl.ds(0, 64)], ups) + both(Q.at[zu, c, pl.ds(64, 64)], downs)
    kg = [both(K.at[a, :, c], other)[0] for a in (z, zd, zu, zf)]
    vg = [both(V.at[a, c], other)[0] for a in (xd, xu, xf)]
    qs = [both(Q.at[a, c], other)[0] for a in (z, zd, zu, zf)]
    oy = both(OC.at[0, y], dict(row=yu), dict(row=yd))
    oyf = both(OC.at[0, yd, pl.ds(0, 1024)], dict(row=yu)) + both(OC.at[0, yu, pl.ds(1024, 1024)], dict(row=yd))
    ow = both(OC.at[1, :, pl.ds(x * 512, 512)], dict(src=su), dict(src=sd))
    owf = both(OC.at[1, pl.ds(0, 2), pl.ds(xd * 512, 512)], dict(src=su)) + both(OC.at[1, pl.ds(2, 2), pl.ds(xu * 512, 512)], dict(src=sd))
    remote = kx + vx + oa + ob + kz + qz[0] + qz[1] + kf + vf + qf + kg + vg + qs + oy + oyf + ow + owf

    def start(*copies):
        for cp in copies:
            cp.start()

    def arrived(*copies):
        for cp in copies:
            cp.wait_recv()

    start(loc_k, *loc_o, loc_v)
    part[...] = jnp.zeros(part.shape, F32)
    pl.semaphore_wait(barrier, 16)
    start(*kx)

    @pl.when(stays)
    def _():
        keep.start()

    @pl.when(jnp.logical_not(stays))
    def _():
        start(*move)
    start(*oa)
    loc_k.wait()
    arrived(*kx)
    start(*kz, kg[0])
    start(*ob, *vx)

    @pl.when(stays)
    def _():
        keep.wait()

    for h in (0, 1):
        @pl.when(jnp.logical_not(stays))
        def _():
            arrived(move[h])
        start(*qz[h])
    start(qs[0])
    for cp in loc_o:
        cp.wait()
    loc_v.wait()
    arrived(*oa)
    start(*oy)
    arrived(*ob)
    start(*ow)
    for h in (0, 1):
        arrived(kz[h])
        start(kf[h], kg[1 + h])
    for h in (0, 1):
        arrived(vx[h])
        start(vf[h], vg[h])
    arrived(qz[0][0])
    start(qf[0])
    arrived(kg[0], qs[0])

    jl = lax.broadcasted_iota(jnp.int32, (128, 256), 0)
    il = lax.broadcasted_iota(jnp.int32, (128, 256), 1) % 128

    def scores(zc, slot, ib, base):
        MS[...] = jnp.full(MS.shape, NEG, F32)
        LS[...] = jnp.zeros(LS.shape, F32)

        def block(jb, diag):
            for hp in range(8):
                kk = K[zc, jb // 2, jb % 2, :, (hp // 4) * 128:(hp // 4 + 1) * 128]
                qq = jnp.concatenate([Q[zc, slot, :, (2 * hp + a) * 128:(2 * hp + a + 1) * 128] for a in (0, 1)], axis=0)
                sc = lax.dot_general(kk, qq, (((1,), (1,)), ((), ())), preferred_element_type=F32)
                if diag:
                    sc = jnp.where(jl <= il, sc, NEG)
                m = jnp.max(sc, axis=0, keepdims=True)
                e = jnp.exp2((sc - m) * C2)
                l = jnp.sum(e, axis=0, keepdims=True)
                for a in (0, 1):
                    lanes = slice(a * 128, (a + 1) * 128)
                    P[jb, pl.ds(2 * hp + a, 128, stride=PS), :] = e[:, lanes]
                    MS[jb, 2 * hp + a:2 * hp + a + 1, :] = m[:, lanes]
                    LS[jb, 2 * hp + a:2 * hp + a + 1, :] = l[:, lanes]

        def plain(jb, carry):
            block(jb, False)
            return carry
        lax.fori_loop(0, ib, plain, 0)
        block(ib, True)
        ms = MS[...]
        f = jnp.exp2((ms - jnp.max(ms, axis=0, keepdims=True)) * C2)
        total = jnp.sum(f * LS[...], axis=0, keepdims=True)
        FS[...] = f / total

        def conv(jb, carry):
            fs = FS[jb]
            for j in range(128):
                W[base + jb, j, pl.ds(pl.multiple_of(zc * 16, 16), 16), :] = (P[jb, j * PS:j * PS + 16, :] * fs).astype(BF)
            return carry
        lax.fori_loop(0, ib + 1, conv, 0)

    turn = (x * (big + 1)) // 4

    def source(t):
        return jnp.where(t + turn > big, t + turn - big - 1, t + turn)

    def images(t):
        jb = source(t)
        for h in range(64):
            vv = V[jb // 2, jb % 2, :, (h // 8) * 128:(h // 8 + 1) * 128]
            oo = jnp.concatenate([OC[a, h // 16, (h % 16) * 128:(h % 16 + 1) * 128, :] for a in (0, 1)], axis=1)
            im = jnp.dot(vv, oo, preferred_element_type=F32)
            for a in (0, 1):
                IM[a, pl.ds(h, 128, stride=IS), :] = im[:, a * 128:(a + 1) * 128]

    def zstep(d, carry):
        @pl.when(d == 1)
        def _():
            arrived(qz[0][1], qz[1][1])
            start(qf[1], qs[2])
            arrived(qz[1][0])
            start(qs[1])
            for h in (0, 1):
                arrived(oy[h])
                start(oyf[h])
            for h in (0, 1):
                arrived(ow[h])
                start(owf[h])
            arrived(kg[1], qs[1])

        @pl.when(d == 2)
        def _():
            arrived(*kf)
            start(kg[3])
            arrived(*vf)
            start(vg[2])
            arrived(kg[2], qs[2])

        @pl.when(d == 3)
        def _():
            arrived(*qf)
            start(qs[3])
            arrived(kg[3], vx[2], *vg, *oyf, *owf)
            images(0)
            arrived(qs[3])
        zc = (z + jnp.where(d == 1, 3, jnp.where(d == 2, 1, jnp.where(d == 3, 2, 0)))) % 4
        scores(zc, 0, p, big + 1)
        scores(zc, 1, big, 0)
        return carry
    lax.fori_loop(0, 4, zstep, 0)

    for w in (zu, zd, zf):
        pl.semaphore_signal(ready, inc=1, device_id={**at, "width": w}, device_id_type=MESH)

    def block_to(n):
        return pltpu.make_async_remote_copy(part.at[:, pl.ds(n * 32, 32), :], RB.at[me], rsend.at[n], rrecv, device_id=peer(n), device_id_type=MESH)

    def first_to(d):
        return pltpu.make_async_remote_copy(TL.at[0], TB.at[z], tsend.at[d], trecv.at[d], device_id={**at, "width": (z + d) % 4}, device_id_type=MESH)

    def second_to(d):
        n = (s + d) % 8
        return pltpu.make_async_remote_copy(TL.at[1], TB.at[4 + s], tsend.at[4 + d], trecv.at[4 + d], device_id={"width": z, "row": mixed(p, n // 2), "src": n}, device_id_type=MESH)


    def jstep(t, carry):
        jb = source(t)

        def contrib(t, slot):
            zero = jnp.zeros((64, 128), BF)
            PU = 64

            def pairs(n, carry):
                got = []
                for u in range(PU):
                    j = n * (2 * PU) + 2 * u
                    r0 = pl.multiple_of(n * (2 * PU * IS), 8)
                    lhs = jnp.concatenate([jnp.concatenate([IM[a, pl.ds(r0 + (2 * u + b) * IS, 64), :].astype(BF) for b in (0, 1)], axis=0) for a in (0, 1)], axis=1)
                    rhs = jnp.concatenate([
                        jnp.concatenate([W[t, j], zero], axis=1),
                        jnp.concatenate([zero, W[t, j + 1]], axis=1)], axis=0)
                    cc = lax.dot_general(lhs, rhs, (((0,), (0,)), ((), ())), preferred_element_type=F32)
                    r = jnp.sum(jnp.abs(cc), axis=0, keepdims=True)
                    got += [r[:, :128], r[:, 128:]]
                for b in range(PU // 4):
                    part[slot, pl.ds(pl.multiple_of(jb * 128 + n * (2 * PU) + 8 * b, 8), 8), :] = jnp.concatenate(got[8 * b:8 * b + 8], axis=0)
                return carry
            lax.fori_loop(0, 128 // (2 * PU), pairs, 0)
        contrib(jb, 1)

        @pl.when(jb <= p)
        def _():
            contrib(big + 1 + jb, 0)

        @pl.when(t == 0)
        def _():
            pl.semaphore_wait(ready, 3)

        @pl.when(t == 1)
        def _():
            for cp in remote:
                cp.wait_send()

            @pl.when(jnp.logical_not(stays))
            def _():
                for cp in move:
                    cp.wait_send()
        for w in range(4):
            n = jb * 4 + w

            @pl.when(n != me)
            def _():
                block_to(n).start()

        @pl.when(t < big)
        def _():
            images(t + 1)
        return carry
    lax.fori_loop(0, big + 1, jstep, 0)

    tl = jnp.concatenate([jnp.sum(part[a].reshape(128, 8, 128), axis=0) for a in (0, 1)], axis=0)
    TL[0] = tl
    firsts = [first_to(d) for d in range(1, 4)]
    seconds = [second_to(d) for d in range(1, 8)]
    start(*firsts)
    TB[z] = tl

    @pl.when(s <= big)
    def _():
        RB[me] = part[:, pl.ds(pl.multiple_of(me * 32, 32), 32), :]
    arrived(*firsts)
    tl = jnp.sum(TB[0:4], axis=0)
    TL[1] = tl
    start(*seconds)
    TB[4 + s] = tl

    def sent(n, carry):
        @pl.when(n != me)
        def _():
            block_to(n).wait_send()
        return carry

    def scale(tb, a, ib):
        total = jnp.sum(tb[8 * a:8 * a + 8], axis=0, keepdims=True)
        pos = (ib * 128 + 1 + lax.broadcasted_iota(jnp.int32, (1, 128), 1)).astype(F32)
        return pos / total

    @pl.when(s <= big)
    def _():
        pltpu.make_async_remote_copy(RB.at[pl.ds(0, 31)], RB.at[pl.ds(0, 31)], rsend.at[0], rrecv, device_id=at, device_id_type=MESH).wait_recv()
        NB[...] = jnp.sum(RB[...], axis=0)

    @pl.when(s > big)
    def _():
        NB[...] = jnp.zeros(NB.shape, F32)
    arrived(*seconds)
    tb = jnp.sum(TB[4:12], axis=0)
    for a, ib in ((0, p), (1, big)):
        NB[a] = NB[a] * scale(tb, a, ib)

    def home(a):
        ib = (p, big)[a]
        return ib // 2, ib % 2, pltpu.make_async_remote_copy(NB.at[a], out.at[ib % 2], wsend.at[a], wrecv.at[ib % 2], device_id={**at, "row": ib // 2}, device_id_type=MESH)

    for a in (0, 1):
        owner, half, cp = home(a)

        @pl.when(owner == y)
        def _():
            out[half] = NB[a]

        @pl.when(owner != y)
        def _():
            cp.start()
    lax.fori_loop(0, (big + 1) * 4, sent, 0)
    for cp in firsts + seconds:
        cp.wait_send()
    for h in (0, 1):
        ib = y * 2 + h
        came = mixed(jnp.where(ib < 4, ib, 7 - ib), x)

        @pl.when(came != y)
        def _():
            pltpu.make_async_remote_copy(NB.at[h], out.at[h], wsend.at[h], wrecv.at[h], device_id={**at, "row": came}, device_id_type=MESH).wait_recv()
    for a in (0, 1):
        owner, half, cp = home(a)

        @pl.when(owner != y)
        def _():
            cp.wait_send()


def body(query_rows, key_rows, value_rows, out_proj):
    hbm = pl.BlockSpec(memory_space=pl.ANY)
    D = pltpu.SemaphoreType.DMA
    out = pl.pallas_call(
        layer_kernel, out_shape=jax.ShapeDtypeStruct((2, 32, 128), F32), in_specs=[hbm] * 4,
        out_specs=pl.BlockSpec(memory_space=pltpu.VMEM),
        scratch_shapes=[
            pltpu.VMEM((4, 2, 128, 2048), BF), pltpu.VMEM((4, 4, 2, 128, 256), BF), pltpu.VMEM((4, 2, 128, 1024), BF), pltpu.VMEM((2, 4, 2048, 128), BF),
            *SCR, pltpu.VMEM((2, 1024, 128), F32), pltpu.VMEM((32, 2, 32, 128), F32), pltpu.VMEM((12, 16, 128), F32),
            pltpu.VMEM((2, 16, 128), F32), pltpu.VMEM((2, 32, 128), F32),
            D((80,)), D((80,)), D((8,)), D((32,)), D, D((12,)), D((12,)), D((2,)), D((2,)), pltpu.SemaphoreType.REGULAR],
        compiler_params=pltpu.CompilerParams(collective_id=0, has_side_effects=True, vmem_limit_bytes=62 * 2**20),
    )(query_rows, key_rows, value_rows, out_proj)
    return out.transpose(0, 2, 1).reshape(256, 32)


def solution(mesh):
    placed = (PS_("row", "width"), PS_("src", "width"), PS_("src", None), PS_(("row", "src"), "width"))
    return jax.shard_map(
        body, mesh=mesh, in_specs=placed, out_specs=PS_("row", ("src", "width")), check_vma=False
    )
```
